32 devices in a mesh: dom: 4 (over y, x), freq: 8 (over z, core).
Axes of the slice: x: 2, y: 2, z: 4, core: 2. Of those that a mesh axis runs over, the one named last changes fastest.
Arguments:
- voltages: float32 [512, 8192], P('freq', 'dom'), may hold values from -5 to 5
- sources: float32 [512, 8192], P('freq', 'dom'), may hold values from -20 to 20
- terminals: int32 [2, 16384], P(None, 'dom'), may hold values from 0 to 2559, as said below
- elem_current: float32 [2, 16384], P(None, 'dom'), may hold values from 0.2 to 2
- elem_charge: float32 [2, 16384], P(None, 'dom'), may hold values from 0.1 to 1
- jacobi: float32 [256, 2, 2, 8192], P('freq', None, None, 'dom'), may hold values from -1.2 to 2
Outputs:
- residual: float32 [512, 8192], P('freq', 'dom')
- newton_step: float32 [512, 8192], P('freq', 'dom')
- residual_norm: float32 [], replicated
The draws below stay inside these ranges and needn't reach their ends.
Inputs may be any that keep to these rules, and one draw needn't show every extreme that they name: `terminals`: A terminal value below 2048 is a node of the element's own partition; a value v of 2048 or more is node (v - 2048) % 128 of partition (v - 2048) // 128, one of that partition's first 128 nodes.
All inputs are finite; a program needn't handle non-finite values.
Results may differ from the reference program's by a relative error of at most 0.0003.
Values sent between devices are 32-bit elements; how exact they have to be, the bound alone decides.
A program may use at most 64 MiB of HBM per device.

```python
import math
import jax
import jax.numpy as jnp
from jax import lax

S = 512
NPD = 2048
NE = 4096
NB = 128
H = 256
NODES = 8192
NBT = 512
ELEMS = 16384
N_DOM = 4


def draw_terminals(key, part):
    first_key, other_key, remote_key, pick_key = jax.random.split(key, 4)
    first = jax.random.randint(first_key, (ELEMS,), 0, NPD)
    local_other = jax.random.randint(other_key, (ELEMS,), 0, NPD)
    remote = NPD + jax.random.randint(remote_key, (ELEMS,), 0, NBT)
    picked = jax.random.randint(pick_key, (ELEMS,), 0, 4) == 0
    second = jnp.where(picked, remote, local_other)
    first = first.at[0].set(0)
    second = second.at[0].set(NPD + NBT - 1)
    return jnp.stack([first, second]).astype(jnp.int32)


def draw_sources(key, part):
    base_key = jax.random.fold_in(key, 0)
    rows = jnp.arange(S, dtype=jnp.float32) / (S - 1)
    columns = jnp.arange(NODES, dtype=jnp.float32) / (NODES - 1)
    scale = 0.5 * (1.0 + 2.0 * rows)[:, None] * (1.0 + 2.0 * columns)[None, :]
    base = jax.random.truncated_normal(base_key, -4.0, 4.0, (S, NODES), jnp.float32)
    return (base * scale).astype(jnp.float32)


def draw_jacobi(key, part):
    keys = jax.random.split(key, 6)
    shape = (H, NODES)
    bottom = 0.5
    top = 2.0
    low_off = 0.25
    high_off = 0.6
    diag_one = jnp.exp(jax.random.uniform(keys[0], shape, jnp.float32, math.log(bottom), math.log(top)))
    diag_two = jnp.exp(jax.random.uniform(keys[1], shape, jnp.float32, math.log(bottom), math.log(top)))
    mix_one = jax.random.uniform(keys[2], shape, jnp.float32, low_off, high_off)
    mix_two = jax.random.uniform(keys[3], shape, jnp.float32, low_off, high_off)
    sign_one = jnp.where(jax.random.randint(keys[4], shape, 0, 2) == 0, -1.0, 1.0)
    sign_two = jnp.where(jax.random.randint(keys[5], shape, 0, 2) == 0, -1.0, 1.0)
    mean_diag = jnp.sqrt(diag_one * diag_two)
    off_one = sign_one * mix_one * mean_diag
    off_two = sign_two * mix_two * mean_diag
    upper = jnp.stack([diag_one, off_one], axis=1)
    lower = jnp.stack([off_two, diag_two], axis=1)
    return jnp.stack([upper, lower], axis=1).astype(jnp.float32)


def levels(stream_key, dims, cuts, least, largest):
    def one(axis_at, parts):
        heights = jax.random.uniform(jax.random.fold_in(jax.random.fold_in(stream_key, 6), axis_at), (parts,), jnp.float32, least / len(cuts), largest / len(cuts))
        return jnp.repeat(jnp.exp(heights), dims[axis_at] // parts).reshape((-1,) + (1,) * (len(dims) - axis_at - 1))

    gain = one(*cuts[0])
    for cut in cuts[1:]:
        gain = gain * one(*cut)
    return gain


def noise(key, extent, deviation, bound, cuts=(), held_as=jnp.bfloat16):
    level = levels(key, extent, cuts, -0.22, 0.18) if cuts else 1.0
    drawn = jax.random.normal(key, extent, jnp.float32) * deviation * level
    return jnp.minimum(jnp.maximum(drawn, -bound), bound).astype(held_as)


def setup_inputs(seed: int = 0) -> dict:
    splits = jax.random.split(jax.random.key(seed), 7)
    return {
        "voltages": noise(splits[0], (S, NODES), 1.0, 5.0, ((0, 8), (1, 4)), jnp.float32),
        "sources": draw_sources(jax.random.fold_in(splits[6], 71), 0),
        "terminals": draw_terminals(jax.random.fold_in(splits[6], 71), 0),
        "elem_current": jnp.clip(jnp.exp(math.log(2.0) - 2.3025851 * jax.random.uniform(splits[3], (2, ELEMS), jnp.float32) ** levels(splits[3], (2, ELEMS), ((1, 4),), -0.2, 0.2)), 0.2, 2.0),
        "elem_charge": jnp.clip(jnp.exp(math.log(1.0) - 2.3025851 * jax.random.uniform(splits[4], (2, ELEMS), jnp.float32) ** levels(splits[4], (2, ELEMS), ((1, 4),), -0.2, 0.2)), 0.1, 1.0),
        "jacobi": draw_jacobi(jax.random.fold_in(splits[6], 71), 0),
    }


trust_radius = 2.0

def transform_table(samples):
    row_index = jnp.arange(samples, dtype=jnp.int32)
    harmonic = row_index // 2
    is_sine = row_index % 2 == 1
    column = jnp.arange(samples, dtype=jnp.int32)
    order = jnp.where(harmonic == 0, jnp.where(is_sine, samples // 2, 0), harmonic)
    phase = (order[:, None] * column[None, :] % samples).astype(jnp.float32) * (2.0 * math.pi / samples)
    use_sine = is_sine & (harmonic > 0)
    values = jnp.where(use_sine[:, None], jnp.sin(phase), jnp.cos(phase))
    weight = jnp.where(harmonic == 0, math.sqrt(1.0 / samples), math.sqrt(2.0 / samples)).astype(jnp.float32)
    forward = values * weight[:, None]
    pairs = forward.reshape(samples // 2, 2, samples)
    rate = 2.0 / samples * jnp.arange(samples // 2, dtype=jnp.float32)
    derived = jnp.stack([pairs[:, 1], -pairs[:, 0]], axis=1) * rate[:, None, None]
    return jnp.concatenate([forward, derived.reshape(samples, samples)], axis=1)

def reference(voltages, sources, terminals, elem_current, elem_charge, jacobi):
    node_total = voltages.shape[1]

    def partition(totals, index):
        local_terms = lax.dynamic_slice_in_dim(terminals, index * NE, NE, 1)
        cur_params = lax.dynamic_slice_in_dim(elem_current, index * NE, NE, 1)
        chg_params = lax.dynamic_slice_in_dim(elem_charge, index * NE, NE, 1)
        border_id = local_terms - NPD
        remote = border_id // NB * NPD + border_id % NB
        global_terms = jnp.where(local_terms < NPD, index * NPD + local_terms, remote).astype(jnp.int32)
        across = voltages[:, global_terms[0]] - voltages[:, global_terms[1]]
        current = cur_params[0][None, :] * across + cur_params[1][None, :] * jnp.tanh(2.0 * across)
        charge = chg_params[0][None, :] * across + chg_params[1][None, :] * jnp.tanh(across)
        flows = jnp.stack([current, charge])
        totals = totals.at[:, :, global_terms[0]].add(flows)
        totals = totals.at[:, :, global_terms[1]].add(-flows)
        return (totals, None)
    start = jnp.zeros((2, S, node_total), jnp.float32)
    totals, unused = lax.scan(partition, start, jnp.arange(N_DOM, dtype=jnp.int32))
    table = transform_table(S)
    stacked = totals.reshape(2 * S, node_total)
    residual = jnp.dot(table, stacked, precision=lax.Precision.HIGHEST, preferred_element_type=jnp.float32) - sources
    pairs = residual.reshape(S // 2, 2, node_total)
    raw = -(jacobi[:, :, 0, :] * pairs[:, 0:1, :] + jacobi[:, :, 1, :] * pairs[:, 1:2, :])
    raw = raw.reshape(S, node_total)
    squares = jnp.sum(raw * raw)
    spread = jnp.sqrt(squares / (S * node_total) + 1e-06)
    newton_step = raw * jnp.minimum(1.0, trust_radius / spread)
    residual_norm = jnp.sqrt(jnp.sum(residual * residual))
    return (residual, newton_step, residual_norm)
```

```python
import functools
import math

import jax
import jax.numpy as jnp
import numpy as np
from jax import lax
from jax.experimental import pallas as pl
from jax.experimental.pallas import tpu as pltpu
from jax.sharding import PartitionSpec as P

MESH = pl.DeviceIdType.MESH
LANES = 128
VMEM = pltpu.VMEM
trust_radius = 2.0
TOLERANCE = 5e-7


def fourier_tables(samples):
    row = np.arange(samples)
    harmonic = row // 2
    sine = row % 2 == 1
    order = np.where(harmonic == 0, np.where(sine, samples // 2, 0), harmonic)
    phase = (order[:, None] * np.arange(samples)[None, :] % samples) * (2.0 * math.pi / samples)
    values = np.where((sine & (harmonic > 0))[:, None], np.sin(phase), np.cos(phase))
    weight = np.where(harmonic == 0, math.sqrt(1.0 / samples), math.sqrt(2.0 / samples))
    full = values * weight[:, None]
    pairs = full.reshape(samples // 2, 2, samples)
    rate = (2.0 / samples) * np.arange(samples // 2)
    derived = np.stack([pairs[:, 1], -pairs[:, 0]], axis=1) * rate[:, None, None]
    return full, derived.reshape(samples, samples)


def split_table(full):
    full = full.astype(np.float32)
    high = full.astype(jnp.bfloat16)
    low = (full - high.astype(np.float32)).astype(jnp.bfloat16)
    return high, low


def up(value, step):
    return -(-value // step) * step


def exchange_tables(samples, chips):
    full, derived = fourier_tables(samples)
    own = samples // chips
    part = own // 2
    blocks, rank = {}, 0
    for k in range(chips):
        for m in range(chips):
            rows, first, second = slice(m * own, (m + 1) * own), k * own, k * own + part
            block = np.concatenate(
                [t[rows, s : s + part] for s in (first, second) for t in (full, derived)], axis=1
            )
            blocks[m, k] = block
            if m != k:
                values = np.linalg.svd(block, compute_uv=False)
                rank = max(rank, int((values > TOLERANCE * values[0]).sum()))
    rank = up(rank, 8)
    stride = up(rank, 16)
    encode = np.zeros((chips, own + (chips - 1) * stride, 2 * own))
    decode = np.zeros((chips, own, (chips - 1) * stride))
    for k in range(chips):
        encode[k, :own] = blocks[k, k]
        for j in range(1, chips):
            start = (j - 1) * stride
            left, values, right = np.linalg.svd(blocks[k ^ j, k], full_matrices=False)
            encode[k, own + start : own + start + rank] = values[:rank, None] * right[:rank]
            decode[k ^ j, :, start : start + rank] = left[:, :rank]
    return split_table(encode), split_table(decode), rank, stride


def split(x):
    high = x.astype(jnp.bfloat16)
    low = (x - high.astype(jnp.float32)).astype(jnp.bfloat16)
    return high, low


def dot(a, b, contract=((1,), (0,))):
    return lax.dot_general(a, b, (contract, ((), ())), preferred_element_type=jnp.float32)


def xor(a, b, count):
    out, bit = 0, 1
    while bit < count:
        out = out + bit * ((a // bit + b // bit) % 2)
        bit *= 2
    return out


def kernel(
    doms, freqs, entries, rank, stride,
    v_ref, term_ref, cur_ref, chg_ref, src_any, jac_any, eh_any, el_any, dh_any, dl_any,
    out_any, norm_ref, scale_ref,
    back, raw_ref, volt, seen, inc, partial, flow, stage, land, edge_out, edge, coef, code_out, code,
    src_ref, jac_ref, eh_ref, el_ref, dh_ref, dl_ref, part_dom, part_freq,
    v_send, v_recv, edge_send, edge_recv, core_send, core_recv, code_send, code_recv, back_send, back_recv,
    pd_send, pd_recv, pf_send, pf_recv, load_sem, store_sem,
):
    dom = lax.axis_index("dom")
    freq = lax.axis_index("freq")
    rows, nodes = v_ref.shape
    wide, elems = inc.shape
    border = seen.shape[2]
    chips = freqs // 2
    chip = freq // 2
    core = freq % 2
    other = 1 - core
    half = nodes // 2
    ew = 512
    kb = 256
    one, zero = jnp.bfloat16(1.0), jnp.bfloat16(0.0)

    barrier = pltpu.get_barrier_semaphore()
    for j in range(1, doms):
        pl.semaphore_signal(barrier, inc=1, device_id={"dom": xor(dom, j, doms)}, device_id_type=MESH)
    for j in range(1, freqs):
        pl.semaphore_signal(barrier, inc=1, device_id={"freq": xor(freq, j, freqs)}, device_id_type=MESH)

    loads = [
        pltpu.make_async_copy(a, b, load_sem.at[i])
        for i, (a, b) in enumerate(
            (
                (eh_any.at[chip], eh_ref), (el_any.at[chip], el_ref),
                (dh_any.at[chip], dh_ref), (dl_any.at[chip], dl_ref),
                (src_any, src_ref), (jac_any, jac_ref),
            )
        )
    ]
    for load in loads:
        load.start()

    def dom_copy(j, source, target, send, recv, sender):
        return pltpu.make_async_remote_copy(
            src_ref=source,
            dst_ref=target.at[sender],
            send_sem=send.at[j],
            recv_sem=recv.at[sender],
            device_id={"dom": xor(dom, j, doms)},
            device_id_type=MESH,
        )

    def v_copy(j, sender):
        return dom_copy(j, v_ref.at[:, :border], seen, v_send, v_recv, sender)

    def edge_copy(j, owner, sender):
        return dom_copy(j, edge_out.at[owner], edge, edge_send, edge_recv, sender)

    if stride > rank:
        for j in range(1, chips):
            gap = (code.shape[0], stride - rank, code.shape[2])
            code[:, j * stride - gap[1] : j * stride] = jnp.zeros(gap, jnp.float32)

    high, low = split(v_ref[...])
    volt[:rows, :nodes] = high
    volt[rows:, :nodes] = low

    def build(i, carry):
        @pl.when(i == 1)
        def _():
            pl.semaphore_wait(barrier, doms + freqs - 2)
            for j in range(doms - 1, 0, -1):
                v_copy(j, dom).start()

        cols = pl.ds(pl.multiple_of(i * ew, ew), ew)
        first = term_ref[0:1, cols]
        second = term_ref[1:2, cols]
        same = first == second
        first = jnp.where(same, -1, first)
        second = jnp.where(same, -1, second)
        total = jnp.zeros((2 * rows, ew), jnp.float32)
        base = lax.broadcasted_iota(jnp.int16, (kb, ew), 0)
        for k in range(wide // kb):
            plus = base == (first - k * kb).astype(jnp.int16)
            minus = base == (second - k * kb).astype(jnp.int16)
            tile = jnp.where(plus, one, jnp.where(minus, -one, zero))
            inc[k * kb : (k + 1) * kb, cols] = tile
            if k * kb < nodes:
                total = total + dot(volt[:, k * kb : (k + 1) * kb], tile)
        partial[:, cols] = total[:rows] + total[rows:]
        return carry

    lax.fori_loop(0, elems // ew, build, 0)

    seen[dom] = v_ref[:, :border]
    for j in range(1, doms):
        v_copy(j, xor(dom, j, doms)).wait_recv()
    for p in range(doms):
        high, low = split(seen[p])
        volt[:rows, nodes + p * border : nodes + (p + 1) * border] = high
        volt[rows:, nodes + p * border : nodes + (p + 1) * border] = low

    def evaluate(i, carry):
        cols = pl.ds(pl.multiple_of(i * ew, ew), ew)
        total = dot(volt[:, nodes:], inc[nodes:, cols])
        across = partial[:, cols] + (total[:rows] + total[rows:])
        current = cur_ref[0:1, cols] * across + cur_ref[1:2, cols] * jnp.tanh(2.0 * across)
        charge = chg_ref[0:1, cols] * across + chg_ref[1:2, cols] * jnp.tanh(across)
        high, low = split(current)
        flow[:rows, cols] = high
        flow[rows : 2 * rows, cols] = low
        high, low = split(charge)
        flow[2 * rows : 3 * rows, cols] = high
        flow[3 * rows :, cols] = low
        return carry

    lax.fori_loop(0, elems // ew, evaluate, 0)

    blocks = half // kb
    own = 2 * rows
    per = kb // border

    def scatter(start):
        total = dot(flow[...], inc[pl.ds(pl.multiple_of(start, LANES), kb), :], ((1,), (1,)))
        current = total[:rows] + total[rows : 2 * rows]
        charge = total[2 * rows : 3 * rows] + total[3 * rows :]
        return jnp.concatenate([current, charge], axis=0)

    def border_block(i, carry):
        piece = scatter(nodes + i * kb)
        for c in range(per):
            edge_out[i * per + c] = piece[:, c * border : (c + 1) * border]
        return carry

    def samples_of(which):
        return pl.ds(pl.multiple_of(which * own, own), own)

    def rows_of(which):
        return pl.ds(pl.multiple_of(which * rows, rows), rows)

    def columns_of(which, b):
        return pl.ds(pl.multiple_of(which * half + b * kb, kb), kb)

    def core_copy(b, sender):
        return pltpu.make_async_remote_copy(
            src_ref=stage.at[b],
            dst_ref=land.at[b, samples_of(sender)],
            send_sem=core_send.at[b],
            recv_sem=core_recv.at[b],
            device_id={"freq": chip * 2 + other},
            device_id_type=MESH,
        )

    def code_copy(b, j):
        piece = pl.ds((j - 1) * stride, rank)
        return pltpu.make_async_remote_copy(
            src_ref=code_out.at[b, piece],
            dst_ref=code.at[b, piece],
            send_sem=code_send.at[b, j],
            recv_sem=code_recv.at[b, j],
            device_id={"freq": xor(chip, j, chips) * 2 + core},
            device_id_type=MESH,
        )

    def back_copy(b, sender):
        return pltpu.make_async_remote_copy(
            src_ref=coef.at[b, rows_of(other)],
            dst_ref=back.at[:, columns_of(sender, b)],
            send_sem=back_send.at[b],
            recv_sem=back_recv.at[b],
            device_id={"freq": chip * 2 + other},
            device_id_type=MESH,
        )

    def product(high, low, x):
        x_high, x_low = split(x)
        return dot(high, x_high) + (dot(high, x_low) + dot(low, x_high))

    for load in loads:
        load.wait()

    far = sorted(range(1, chips), key=lambda j: -j)

    def node_block(i, carry):
        b = blocks - 1 - i
        last = i == blocks - 1

        @pl.when(last)
        def _():
            for k in range(1, doms):
                edge_copy(k, dom, xor(dom, k, doms)).wait_recv()
            total = edge_out[dom]
            for p in range(doms):
                total = total + jnp.where(dom == p, 0.0, edge[p])
            edge_out[dom] = total

        stage[b] = scatter(other * half + b * kb)

        @pl.when(jnp.logical_and(last, core == 1))
        def _():
            stage[0, :, :border] = stage[0, :, :border] + edge_out[dom]

        core_copy(b, core).start()
        land[b, samples_of(core)] = scatter(core * half + b * kb)

        @pl.when(jnp.logical_and(last, core == 0))
        def _():
            land[0, :own, :border] = land[0, :own, :border] + edge_out[dom]

        core_copy(b, other).wait_recv()
        result = product(eh_ref[...], el_ref[...], land[b])
        coef[b] = result[:own]
        code_out[b] = result[own:]
        for j in far:
            code_copy(b, j).start()

        @pl.when(i == 0)
        def _():
            lax.fori_loop(0, (wide - nodes) // kb, border_block, 0)
            for k in range(doms - 1, 0, -1):
                edge_copy(k, xor(dom, k, doms), dom).start()

        return carry

    lax.fori_loop(0, blocks, node_block, 0)

    def join(b):
        for j in far:
            code_copy(b, j).wait_recv()
        coef[b] = coef[b] + product(dh_ref[...], dl_ref[...], code[b])
        back_copy(b, core).start()
        back[:, columns_of(core, b)] = coef[b, rows_of(core)]

    even = lax.broadcasted_iota(jnp.int32, (rows, LANES), 0) % 2 == 0

    def fold(x):
        return jnp.sum((x * x).reshape(rows // 8, 8, LANES), axis=0)

    def finish(b, sums):
        back_copy(b, other).wait_recv()

        def piece(i, carry):
            start = (i // (kb // LANES)) * half + b * kb + (i % (kb // LANES)) * LANES
            cols = pl.ds(pl.multiple_of(start, LANES), LANES)
            residual = back[:, cols] - src_ref[:, cols]
            upper = jnp.where(even, residual, pltpu.roll(residual, 1, 0))
            lower = jnp.where(even, pltpu.roll(residual, rows - 1, 0), residual)
            raw = -(jac_ref[:, 0, cols] * upper + jac_ref[:, 1, cols] * lower)
            back[:, cols] = residual
            raw_ref[:, cols] = raw
            return carry[0] + fold(raw), carry[1] + fold(residual)

        return lax.fori_loop(0, 2 * (kb // LANES), piece, sums)

    zeros = jnp.zeros((8, LANES), jnp.float32)

    def close(i, sums):
        b = blocks - 1 - i
        join(b)
        return lax.cond(i > 0, lambda s: finish(b + 1, s), lambda s: s, sums)

    sums = finish(0, lax.fori_loop(0, blocks, close, (zeros, zeros)))

    stores = [
        pltpu.make_async_copy(a, out_any.at[i], store_sem.at[i]) for i, a in enumerate((back, raw_ref))
    ]
    for store in stores:
        store.start()

    def whole(x):
        return jnp.sum(jnp.sum(x, axis=0, keepdims=True), axis=1, keepdims=True)

    lane = lax.broadcasted_iota(jnp.int32, (8, LANES), 1)
    part_dom[dom] = jnp.where(lane == 0, whole(sums[0]), jnp.where(lane == 1, whole(sums[1]), 0.0))

    def part_copy(axis, count, me, part, send, recv, j, sender):
        return pltpu.make_async_remote_copy(
            src_ref=part.at[me],
            dst_ref=part.at[sender],
            send_sem=send.at[j],
            recv_sem=recv.at[sender],
            device_id={axis: xor(me, j, count)},
            device_id_type=MESH,
        )

    def reduce_over(axis, count, me, part, send, recv):
        for j in range(count - 1, 0, -1):
            part_copy(axis, count, me, part, send, recv, j, me).start()
        for j in range(count - 1, 0, -1):
            part_copy(axis, count, me, part, send, recv, j, xor(me, j, count)).wait_recv()
        return sum((part[i] for i in range(1, count)), part[0])

    part_freq[freq] = reduce_over("dom", doms, dom, part_dom, pd_send, pd_recv)
    both = reduce_over("freq", freqs, freq, part_freq, pf_send, pf_recv)
    raw_sum = jnp.sum(jnp.where(lane == 0, both, 0.0)[:1], axis=1, keepdims=True)
    res_sum = jnp.sum(jnp.where(lane == 1, both, 0.0)[:1], axis=1, keepdims=True)
    spread = jnp.sqrt(raw_sum / entries + 1e-06)
    scale_ref[...] = jnp.minimum(1.0, trust_radius / spread)
    norm_ref[...] = jnp.sqrt(res_sum)
    for store in stores:
        store.wait()

    for j in range(1, doms):
        v_copy(j, dom).wait_send()
        edge_copy(j, dom, dom).wait_send()
        part_copy("dom", doms, dom, part_dom, pd_send, pd_recv, j, dom).wait_send()

    for b in range(blocks):
        core_copy(b, core).wait_send()
        back_copy(b, core).wait_send()
        for j in far:
            code_copy(b, j).wait_send()

    def drain_parts(i, carry):
        part_copy("freq", freqs, freq, part_freq, pf_send, pf_recv, i + 1, freq).wait_send()
        return carry

    lax.fori_loop(0, freqs - 1, drain_parts, 0)


def damp_kernel(both_ref, scale_ref, residual_ref, step_ref):
    residual_ref[...] = both_ref[0]
    step_ref[...] = both_ref[1] * scale_ref[...]


def body(doms, freqs, voltages, sources, terminals, elem_current, elem_charge, jacobi):
    rows, nodes = voltages.shape
    elems = terminals.shape[1]
    border = nodes // 16
    wide = nodes + doms * border
    samples = rows * freqs
    chips = freqs // 2
    blocks = nodes // 2 // 256
    own = 2 * rows
    f32, bf16 = jnp.float32, jnp.bfloat16
    dma = pltpu.SemaphoreType.DMA
    vmem = pl.BlockSpec(memory_space=VMEM)
    anywhere = pl.BlockSpec(memory_space=pl.ANY)
    encode, decode, rank, stride = exchange_tables(samples, chips)
    codes = (chips - 1) * stride
    both, norm, scale = pl.pallas_call(
        functools.partial(kernel, doms, freqs, float(samples * nodes * doms), rank, stride),
        out_shape=(
            jax.ShapeDtypeStruct((2, rows, nodes), f32),
            jax.ShapeDtypeStruct((1, 1), f32),
            jax.ShapeDtypeStruct((1, 1), f32),
        ),
        in_specs=[vmem] * 4 + [anywhere] * 6,
        out_specs=(anywhere, vmem, vmem),
        scratch_shapes=[
            VMEM((rows, nodes), f32),
            VMEM((rows, nodes), f32),
            VMEM((2 * rows, wide), bf16),
            VMEM((doms, rows, border), f32),
            VMEM((wide, elems), bf16),
            VMEM((rows, elems), f32),
            VMEM((4 * rows, elems), bf16),
            VMEM((blocks, own, 256), f32),
            VMEM((blocks, 2 * own, 256), f32),
            VMEM((doms, own, border), f32),
            VMEM((doms, own, border), f32),
            VMEM((blocks, own, 256), f32),
            VMEM((blocks, codes, 256), f32),
            VMEM((blocks, codes, 256), f32),
            VMEM((rows, nodes), f32),
            VMEM((rows, 2, nodes), f32),
            VMEM((own + codes, 2 * own), bf16),
            VMEM((own + codes, 2 * own), bf16),
            VMEM((own, codes), bf16),
            VMEM((own, codes), bf16),
            VMEM((doms, 8, LANES), f32),
            VMEM((freqs, 8, LANES), f32),
            dma((doms,)), dma((doms,)),
            dma((doms,)), dma((doms,)),
            dma((blocks,)), dma((blocks,)),
            dma((blocks, chips)), dma((blocks, chips)),
            dma((blocks,)), dma((blocks,)),
            dma((doms,)), dma((doms,)),
            dma((freqs,)), dma((freqs,)),
            dma((6,)),
            dma((2,)),
        ],
        compiler_params=pltpu.CompilerParams(
            collective_id=0, has_side_effects=True, vmem_limit_bytes=60 * 1024 * 1024
        ),
    )(
        voltages, terminals, elem_current, elem_charge,
        sources, jacobi.reshape(rows, 2, nodes), *map(jnp.asarray, encode + decode),
    )
    part = pl.BlockSpec((rows // 2, nodes), lambda i: (i, 0))
    residual, step = pl.pallas_call(
        damp_kernel,
        grid=(2,),
        out_shape=(jax.ShapeDtypeStruct((rows, nodes), f32),) * 2,
        in_specs=[
            pl.BlockSpec((2, rows // 2, nodes), lambda i: (0, i, 0)),
            pl.BlockSpec((1, 1), lambda i: (0, 0)),
        ],
        out_specs=(part, part),
    )(both, scale)
    return residual, step, norm.reshape(())


def solution(mesh):
    placed = (
        P("freq", "dom"),
        P("freq", "dom"),
        P(None, "dom"),
        P(None, "dom"),
        P(None, "dom"),
        P("freq", None, None, "dom"),
    )
    return jax.shard_map(
        functools.partial(body, mesh.shape["dom"], mesh.shape["freq"]),
        mesh=mesh,
        in_specs=placed,
        out_specs=(P("freq", "dom"), P("freq", "dom"), P()),
        check_vma=False,
    )
```

```python
import functools
import math

import jax
import jax.numpy as jnp
import numpy as np
from jax import lax
from jax.experimental import pallas as pl
from jax.experimental.pallas import tpu as pltpu
from jax.sharding import PartitionSpec as P

MESH = pl.DeviceIdType.MESH
LANES = 128
VMEM = pltpu.VMEM
trust_radius = 2.0
TOLERANCE = 5e-7


def fourier_tables(samples):
    row = np.arange(samples)
    harmonic = row // 2
    sine = row % 2 == 1
    order = np.where(harmonic == 0, np.where(sine, samples // 2, 0), harmonic)
    phase = (order[:, None] * np.arange(samples)[None, :] % samples) * (2.0 * math.pi / samples)
    values = np.where((sine & (harmonic > 0))[:, None], np.sin(phase), np.cos(phase))
    weight = np.where(harmonic == 0, math.sqrt(1.0 / samples), math.sqrt(2.0 / samples))
    full = values * weight[:, None]
    pairs = full.reshape(samples // 2, 2, samples)
    rate = (2.0 / samples) * np.arange(samples // 2)
    derived = np.stack([pairs[:, 1], -pairs[:, 0]], axis=1) * rate[:, None, None]
    return full, derived.reshape(samples, samples)


def split_table(full):
    full = full.astype(np.float32)
    high = full.astype(jnp.bfloat16)
    low = (full - high.astype(np.float32)).astype(jnp.bfloat16)
    return high, low


def up(value, step):
    return -(-value // step) * step


def exchange_tables(samples, chips):
    full, derived = fourier_tables(samples)
    own = samples // chips
    part = own // 2
    blocks, rank = {}, 0
    for k in range(chips):
        for m in range(chips):
            rows, first, second = slice(m * own, (m + 1) * own), k * own, k * own + part
            block = np.concatenate(
                [t[rows, s : s + part] for s in (first, second) for t in (full, derived)], axis=1
            )
            blocks[m, k] = block
            if m != k:
                values = np.linalg.svd(block, compute_uv=False)
                rank = max(rank, int((values > TOLERANCE * values[0]).sum()))
    rank = up(rank, 8)
    stride = up(rank, 16)
    encode = np.zeros((chips, 2, own + (chips - 1) * stride, 2 * own))
    decode = np.zeros((chips, own, (chips - 1) * stride))
    for k in range(chips):
        encode[k, :, :own] = blocks[k, k]
        for j in range(1, chips):
            start = (j - 1) * stride
            left, values, right = np.linalg.svd(blocks[k ^ j, k], full_matrices=False)
            encode[k, :, own + start : own + start + rank] = values[:rank, None] * right[:rank]
            decode[k ^ j, :, start : start + rank] = left[:, :rank]
    encode[:, 1] = np.roll(encode[:, 1], own, axis=2)
    encode = encode.reshape((2 * chips,) + encode.shape[2:])
    return split_table(encode), split_table(decode), rank, stride


def split(x):
    high = x.astype(jnp.bfloat16)
    low = (x - high.astype(jnp.float32)).astype(jnp.bfloat16)
    return high, low


def dot(a, b, contract=((1,), (0,))):
    return lax.dot_general(a, b, (contract, ((), ())), preferred_element_type=jnp.float32)


def xor(a, b, count):
    out, bit = 0, 1
    while bit < count:
        out = out + bit * ((a // bit + b // bit) % 2)
        bit *= 2
    return out


def kernel(
    doms, freqs, entries, rank, stride,
    v_ref, term_ref, cur_ref, chg_ref, src_any, jac_any, eh_any, el_any, dh_any, dl_any,
    both_ref, norm_ref,
    volt, seen, inc, partial, flow, stage, land, edge, coef, code_out, code,
    src_ref, jac_ref, eh_ref, el_ref, dh_ref, dl_ref, part,
    v_send, v_recv, edge_send, edge_recv, core_send, core_recv, code_send, code_recv, back_send, back_recv,
    part_send, part_recv, load_sem,
):
    dom = lax.axis_index("dom")
    freq = lax.axis_index("freq")
    rows, nodes = v_ref.shape
    wide, elems = inc.shape
    border = seen.shape[2]
    chips = freqs // 2
    chip = freq // 2
    core = freq % 2
    other = 1 - core
    half = nodes // 2
    ew = 512
    kb = 256
    one, zero = jnp.bfloat16(1.0), jnp.bfloat16(0.0)

    barrier = pltpu.get_barrier_semaphore()
    for j in range(1, doms):
        pl.semaphore_signal(barrier, inc=1, device_id={"dom": xor(dom, j, doms)}, device_id_type=MESH)
    for j in range(1, freqs):
        pl.semaphore_signal(barrier, inc=1, device_id={"freq": xor(freq, j, freqs)}, device_id_type=MESH)

    loads = [
        pltpu.make_async_copy(a, b, load_sem.at[i])
        for i, (a, b) in enumerate(
            (
                (eh_any.at[freq], eh_ref), (el_any.at[freq], el_ref),
                (dh_any.at[chip], dh_ref), (dl_any.at[chip], dl_ref),
                (src_any, src_ref), (jac_any, jac_ref),
            )
        )
    ]
    for load in loads:
        load.start()

    def dom_copy(j, source, target, send, recv, sender):
        return pltpu.make_async_remote_copy(
            src_ref=source,
            dst_ref=target.at[sender],
            send_sem=send.at[j],
            recv_sem=recv.at[sender],
            device_id={"dom": xor(dom, j, doms)},
            device_id_type=MESH,
        )

    def v_copy(j, sender):
        return dom_copy(j, v_ref.at[:, :border], seen, v_send, v_recv, sender)

    def edge_copy(j, owner, sender):
        return dom_copy(j, edge_out(owner), edge, edge_send, edge_recv, sender)

    if stride > rank:
        for j in range(1, chips):
            gap = (code.shape[0], stride - rank, code.shape[2])
            code[:, j * stride - gap[1] : j * stride] = jnp.zeros(gap, jnp.float32)

    high, low = split(v_ref[...])
    volt[:rows, :nodes] = high
    volt[rows:, :nodes] = low

    def build(i, carry):
        @pl.when(i == 1)
        def _():
            pl.semaphore_wait(barrier, doms + freqs - 2)
            for j in range(doms - 1, 0, -1):
                v_copy(j, dom).start()

        cols = pl.ds(pl.multiple_of(i * ew, ew), ew)
        first = term_ref[0:1, cols]
        second = term_ref[1:2, cols]
        same = first == second
        first = jnp.where(same, -1, first)
        second = jnp.where(same, -1, second)
        total = jnp.zeros((2 * rows, ew), jnp.float32)
        base = lax.broadcasted_iota(jnp.int16, (kb, ew), 0)
        for k in range(wide // kb):
            plus = base == (first - k * kb).astype(jnp.int16)
            minus = base == (second - k * kb).astype(jnp.int16)
            tile = jnp.where(plus, one, jnp.where(minus, -one, zero))
            inc[k * kb : (k + 1) * kb, cols] = tile
            if k * kb < nodes:
                total = total + dot(volt[:, k * kb : (k + 1) * kb], tile)
        partial[:, cols] = total[:rows] + total[rows:]
        return carry

    lax.fori_loop(0, elems // ew, build, 0)

    seen[dom] = v_ref[:, :border]
    for j in range(1, doms):
        v_copy(j, xor(dom, j, doms)).wait_recv()
    for p in range(doms):
        high, low = split(seen[p])
        volt[:rows, nodes + p * border : nodes + (p + 1) * border] = high
        volt[rows:, nodes + p * border : nodes + (p + 1) * border] = low

    def evaluate(i, carry):
        cols = pl.ds(pl.multiple_of(i * ew, ew), ew)
        total = dot(volt[:, nodes:], inc[nodes:, cols])
        across = partial[:, cols] + (total[:rows] + total[rows:])
        current = cur_ref[0:1, cols] * across + cur_ref[1:2, cols] * jnp.tanh(2.0 * across)
        charge = chg_ref[0:1, cols] * across + chg_ref[1:2, cols] * jnp.tanh(across)
        high, low = split(current)
        flow[:rows, cols] = high
        flow[rows : 2 * rows, cols] = low
        high, low = split(charge)
        flow[2 * rows : 3 * rows, cols] = high
        flow[3 * rows :, cols] = low
        return carry

    lax.fori_loop(0, elems // ew, evaluate, 0)

    blocks = half // kb
    own = 2 * rows
    per = kb // border

    def scatter(start):
        total = dot(flow[...], inc[pl.ds(pl.multiple_of(start, LANES), kb), :], ((1,), (1,)))
        current = total[:rows] + total[rows : 2 * rows]
        charge = total[2 * rows : 3 * rows] + total[3 * rows :]
        return jnp.concatenate([current, charge], axis=0)

    def edge_out(owner):
        cols = pl.ds(pl.multiple_of(owner % per * border, border), border)
        return stage.at[2 * blocks + owner // per, :, cols]

    def rows_of(which):
        return pl.ds(pl.multiple_of(which * rows, rows), rows)

    def columns_of(which, b):
        return pl.ds(pl.multiple_of(which * half + b * kb, kb), kb)

    def core_copy(b):
        return pltpu.make_async_remote_copy(
            src_ref=stage.at[2 * b],
            dst_ref=land.at[b],
            send_sem=core_send.at[b],
            recv_sem=core_recv.at[b],
            device_id={"freq": chip * 2 + other},
            device_id_type=MESH,
        )

    def code_copy(b, j):
        piece = pl.ds((j - 1) * stride, rank)
        return pltpu.make_async_remote_copy(
            src_ref=code_out.at[b, piece],
            dst_ref=code.at[b, piece],
            send_sem=code_send.at[b, j],
            recv_sem=code_recv.at[b, j],
            device_id={"freq": xor(chip, j, chips) * 2 + core},
            device_id_type=MESH,
        )

    def back_copy(b, sender):
        return pltpu.make_async_remote_copy(
            src_ref=coef.at[b, rows_of(other)],
            dst_ref=both_ref.at[0, :, columns_of(sender, b)],
            send_sem=back_send.at[b],
            recv_sem=back_recv.at[b],
            device_id={"freq": chip * 2 + other},
            device_id_type=MESH,
        )

    def product(high, low, x):
        x_high, x_low = split(x)
        return dot(high, x_high) + (dot(high, x_low) + dot(low, x_high))

    for load in loads:
        load.wait()

    far = sorted(range(1, chips), key=lambda j: -j)

    rims = (wide - nodes) // kb

    def node_block(i, carry):
        rim = jnp.logical_and(i >= 2, i < 2 + rims)
        step = jnp.where(i < 2, i, i - rims)
        b = blocks - 1 - step // 2
        mine = step % 2
        side = jnp.where(mine == 1, core, other)
        start = jnp.where(rim, nodes + (i - 2) * kb, side * half + b * kb)
        slot = jnp.where(rim, 2 * blocks + i - 2, 2 * b + mine)
        stage[slot] = scatter(start)

        @pl.when(i == 1 + rims)
        def _():
            for k in range(doms - 1, 0, -1):
                edge_copy(k, xor(dom, k, doms), dom).start()

        @pl.when(i == 2 * (blocks - 1) + rims)
        def _():
            for k in range(1, doms):
                edge_copy(k, dom, xor(dom, k, doms)).wait_recv()

        @pl.when(jnp.logical_and(step >= 2 * (blocks - 1), side == 0))
        def _():
            total = stage[slot, :, :border] + edge_out(dom)[...]
            for p in range(doms):
                total = total + jnp.where(dom == p, 0.0, edge[p])
            stage[slot, :, :border] = total

        @pl.when(jnp.logical_and(jnp.logical_not(rim), mine == 0))
        def _():
            core_copy(b).start()

        @pl.when(jnp.logical_and(jnp.logical_not(rim), mine == 1))
        def _():
            core_copy(b).wait_recv()
            result = product(eh_ref[...], el_ref[...], jnp.concatenate([stage[slot], land[b]], axis=0))
            coef[b] = result[:own]
            code_out[b] = result[own:]
            for j in far:
                code_copy(b, j).start()

        return carry

    lax.fori_loop(0, 2 * blocks + rims, node_block, 0)

    def join(b):
        for j in far:
            code_copy(b, j).wait_recv()
        coef[b] = coef[b] + product(dh_ref[...], dl_ref[...], code[b])
        back_copy(b, core).start()
        both_ref[0, :, columns_of(core, b)] = coef[b, rows_of(core)]

    even = lax.broadcasted_iota(jnp.int32, (rows, LANES), 0) % 2 == 0

    def fold(x):
        return jnp.sum((x * x).reshape(rows // 8, 8, LANES), axis=0)

    def finish(b, sums):
        back_copy(b, other).wait_recv()

        def piece(i, carry):
            start = (i // (kb // LANES)) * half + b * kb + (i % (kb // LANES)) * LANES
            cols = pl.ds(pl.multiple_of(start, LANES), LANES)
            residual = both_ref[0, :, cols] - src_ref[:, cols]
            upper = jnp.where(even, residual, pltpu.roll(residual, 1, 0))
            lower = jnp.where(even, pltpu.roll(residual, rows - 1, 0), residual)
            raw = -(jac_ref[:, 0, cols] * upper + jac_ref[:, 1, cols] * lower)
            both_ref[0, :, cols] = residual
            both_ref[1, :, cols] = raw
            return carry[0] + fold(raw), carry[1] + fold(residual)

        return lax.fori_loop(0, 2 * (kb // LANES), piece, sums)

    zeros = jnp.zeros((8, LANES), jnp.float32)

    def close(i, sums):
        b = blocks - 1 - i
        join(b)
        return lax.cond(i > 0, lambda s: finish(b + 1, s), lambda s: s, sums)

    sums = finish(0, lax.fori_loop(0, blocks, close, (zeros, zeros)))

    def whole(x):
        return jnp.sum(jnp.sum(x, axis=0, keepdims=True), axis=1, keepdims=True)

    lane = lax.broadcasted_iota(jnp.int32, (1, LANES), 1)
    count = doms * freqs
    me = dom * freqs + freq
    part[me] = jnp.where(lane == 0, whole(sums[0]), jnp.where(lane == 1, whole(sums[1]), 0.0))

    def part_copy(j, sending):
        dom_at, freq_at = xor(dom, j // freqs, doms), xor(freq, j % freqs, freqs)
        return pltpu.make_async_remote_copy(
            src_ref=part.at[me],
            dst_ref=part.at[me if sending else dom_at * freqs + freq_at],
            send_sem=part_send.at[j],
            recv_sem=part_recv.at[j],
            device_id={"dom": dom_at, "freq": freq_at},
            device_id_type=MESH,
        )

    for j in range(count - 1, 0, -1):
        part_copy(j, True).start()
    for j in range(count - 1, 0, -1):
        part_copy(j, False).wait_recv()
    total = jnp.sum(part[...], axis=0)
    raw_sum = jnp.sum(jnp.where(lane == 0, total, 0.0), axis=1, keepdims=True)
    res_sum = jnp.sum(jnp.where(lane == 1, total, 0.0), axis=1, keepdims=True)
    spread = jnp.sqrt(raw_sum / entries + 1e-06)
    both_ref[1] = both_ref[1] * jnp.minimum(1.0, trust_radius / spread)
    norm_ref[...] = jnp.sqrt(res_sum)

    for j in range(1, doms):
        v_copy(j, dom).wait_send()
        edge_copy(j, dom, dom).wait_send()

    for b in range(blocks):
        core_copy(b).wait_send()
        back_copy(b, core).wait_send()
        for j in far:
            code_copy(b, j).wait_send()

    for j in range(1, count):
        part_copy(j, True).wait_send()


def place_kernel(both_any, norm_any, residual_any, step_any, out_norm_any, sem):
    copies = [
        pltpu.make_async_copy(a, b, sem.at[i])
        for i, (a, b) in enumerate(
            ((both_any.at[0], residual_any), (both_any.at[1], step_any), (norm_any, out_norm_any))
        )
    ]
    for copy in copies:
        copy.start()
    for copy in copies:
        copy.wait()


def body(doms, freqs, voltages, sources, terminals, elem_current, elem_charge, jacobi):
    rows, nodes = voltages.shape
    elems = terminals.shape[1]
    border = nodes // 16
    wide = nodes + doms * border
    samples = rows * freqs
    chips = freqs // 2
    blocks = nodes // 2 // 256
    own = 2 * rows
    f32, bf16 = jnp.float32, jnp.bfloat16
    dma = pltpu.SemaphoreType.DMA
    vmem = pl.BlockSpec(memory_space=VMEM)
    anywhere = pl.BlockSpec(memory_space=pl.ANY)
    encode, decode, rank, stride = exchange_tables(samples, chips)
    codes = (chips - 1) * stride
    both, norm = pl.pallas_call(
        functools.partial(kernel, doms, freqs, float(samples * nodes * doms), rank, stride),
        out_shape=(
            VMEM((2, rows, nodes), f32),
            jax.ShapeDtypeStruct((1, 1), f32),
        ),
        in_specs=[vmem] * 4 + [anywhere] * 6,
        out_specs=(vmem, vmem),
        scratch_shapes=[
            VMEM((2 * rows, wide), bf16),
            VMEM((doms, rows, border), f32),
            VMEM((wide, elems), bf16),
            VMEM((rows, elems), f32),
            VMEM((4 * rows, elems), bf16),
            VMEM((2 * blocks + doms * border // 256, own, 256), f32),
            VMEM((blocks, own, 256), f32),
            VMEM((doms, own, border), f32),
            VMEM((blocks, own, 256), f32),
            VMEM((blocks, codes, 256), f32),
            VMEM((blocks, codes, 256), f32),
            VMEM((rows, nodes), f32),
            VMEM((rows, 2, nodes), f32),
            VMEM((own + codes, 2 * own), bf16),
            VMEM((own + codes, 2 * own), bf16),
            VMEM((own, codes), bf16),
            VMEM((own, codes), bf16),
            VMEM((doms * freqs, 1, LANES), f32),
            dma((doms,)), dma((doms,)),
            dma((doms,)), dma((doms,)),
            dma((blocks,)), dma((blocks,)),
            dma((blocks, chips)), dma((blocks, chips)),
            dma((blocks,)), dma((blocks,)),
            dma((doms * freqs,)), dma((doms * freqs,)),
            dma((6,)),
        ],
        compiler_params=pltpu.CompilerParams(
            collective_id=0, has_side_effects=True, vmem_limit_bytes=56 * 1024 * 1024
        ),
    )(
        voltages, terminals, elem_current, elem_charge,
        sources, jacobi.reshape(rows, 2, nodes), *map(jnp.asarray, encode + decode),
    )
    residual, step, norm = pl.pallas_call(
        place_kernel,
        out_shape=(
            jax.ShapeDtypeStruct((rows, nodes), f32),
            jax.ShapeDtypeStruct((rows, nodes), f32),
            jax.ShapeDtypeStruct((1, 1), f32),
        ),
        in_specs=[anywhere] * 2,
        out_specs=(anywhere,) * 3,
        scratch_shapes=[dma((3,))],
        compiler_params=pltpu.CompilerParams(vmem_limit_bytes=1024 * 1024),
    )(both, norm)
    return residual, step, norm.reshape(())


def solution(mesh):
    placed = (
        P("freq", "dom"),
        P("freq", "dom"),
        P(None, "dom"),
        P(None, "dom"),
        P(None, "dom"),
        P("freq", None, None, "dom"),
    )
    return jax.shard_map(
        functools.partial(body, mesh.shape["dom"], mesh.shape["freq"]),
        mesh=mesh,
        in_specs=placed,
        out_specs=(P("freq", "dom"), P("freq", "dom"), P()),
        check_vma=False,
    )
```

```python
import functools
import math

import jax
import jax.numpy as jnp
import numpy as np
from jax import lax
from jax.experimental import pallas as pl
from jax.experimental.pallas import tpu as pltpu
from jax.sharding import PartitionSpec as P

MESH = pl.DeviceIdType.MESH
LANES = 128
VMEM = pltpu.VMEM
trust_radius = 2.0
TOLERANCE = 5e-7


def fourier_tables(samples):
    row = np.arange(samples)
    harmonic = row // 2
    sine = row % 2 == 1
    order = np.where(harmonic == 0, np.where(sine, samples // 2, 0), harmonic)
    phase = (order[:, None] * np.arange(samples)[None, :] % samples) * (2.0 * math.pi / samples)
    values = np.where((sine & (harmonic > 0))[:, None], np.sin(phase), np.cos(phase))
    weight = np.where(harmonic == 0, math.sqrt(1.0 / samples), math.sqrt(2.0 / samples))
    full = values * weight[:, None]
    pairs = full.reshape(samples // 2, 2, samples)
    rate = (2.0 / samples) * np.arange(samples // 2)
    derived = np.stack([pairs[:, 1], -pairs[:, 0]], axis=1) * rate[:, None, None]
    return full, derived.reshape(samples, samples)


def split_table(full):
    full = full.astype(np.float32)
    high = full.astype(jnp.bfloat16)
    low = (full - high.astype(np.float32)).astype(jnp.bfloat16)
    return high, low


def up(value, step):
    return -(-value // step) * step


def exchange_tables(samples, chips):
    full, derived = fourier_tables(samples)
    own = samples // chips
    part = own // 2
    blocks, rank = {}, 0
    for k in range(chips):
        for m in range(chips):
            rows, first, second = slice(m * own, (m + 1) * own), k * own, k * own + part
            block = np.concatenate(
                [t[rows, s : s + part] for s in (first, second) for t in (full, derived)], axis=1
            )
            blocks[m, k] = block
            if m != k:
                values = np.linalg.svd(block, compute_uv=False)
                rank = max(rank, int((values > TOLERANCE * values[0]).sum()))
    rank = up(rank, 8)
    stride = up(rank, 16)
    encode = np.zeros((chips, 2, own + (chips - 1) * stride, 2 * own))
    decode = np.zeros((chips, own, (chips - 1) * stride))
    for k in range(chips):
        encode[k, :, :own] = blocks[k, k]
        for j in range(1, chips):
            start = (j - 1) * stride
            left, values, right = np.linalg.svd(blocks[k ^ j, k], full_matrices=False)
            encode[k, :, own + start : own + start + rank] = values[:rank, None] * right[:rank]
            decode[k ^ j, :, start : start + rank] = left[:, :rank]
    encode[:, 1] = np.roll(encode[:, 1], own, axis=2)
    encode = encode.reshape((2 * chips,) + encode.shape[2:])
    return split_table(encode), split_table(decode), rank, stride


def split(x):
    high = x.astype(jnp.bfloat16)
    low = (x - high.astype(jnp.float32)).astype(jnp.bfloat16)
    return high, low


def dot(a, b, contract=((1,), (0,))):
    return lax.dot_general(a, b, (contract, ((), ())), preferred_element_type=jnp.float32)


def xor(a, b, count):
    out, bit = 0, 1
    while bit < count:
        out = out + bit * ((a // bit + b // bit) % 2)
        bit *= 2
    return out


def kernel(
    doms, freqs, entries, rank, stride,
    v_any, term_any, cur_any, chg_any, src_any, jac_any, eh_any, el_any, dh_any, dl_any,
    both_ref, norm_ref,
    volt, seen, inc, partial, flow, stage, land, edge, coef, code_out, code,
    v_ref, term_ref, cur_ref, chg_ref, src_ref, jac_ref, eh_ref, el_ref, dh_ref, dl_ref, part,
    v_send, v_recv, edge_send, edge_recv, core_send, core_recv, code_send, code_recv, back_send, back_recv,
    part_send, part_recv, load_sem,
):
    dom = lax.axis_index("dom")
    freq = lax.axis_index("freq")
    rows, nodes = v_ref.shape
    wide, elems = inc.shape
    border = seen.shape[2]
    chips = freqs // 2
    chip = freq // 2
    core = freq % 2
    other = 1 - core
    half = nodes // 2
    bw = min(2048, elems)
    ew = min(2048, elems)
    kb = 256
    one, zero = jnp.bfloat16(1.0), jnp.bfloat16(0.0)

    loads = [
        pltpu.make_async_copy(a, b, load_sem.at[i])
        for i, (a, b) in enumerate(
            (
                (term_any, term_ref), (v_any, v_ref), (cur_any, cur_ref), (chg_any, chg_ref),
                (eh_any.at[freq], eh_ref), (el_any.at[freq], el_ref),
                (dh_any.at[chip], dh_ref), (dl_any.at[chip], dl_ref),
                (src_any, src_ref), (jac_any, jac_ref),
            )
        )
    ]
    for load in loads[:4]:
        load.start()

    barrier = pltpu.get_barrier_semaphore()
    for j in range(1, doms):
        pl.semaphore_signal(barrier, inc=1, device_id={"dom": xor(dom, j, doms)}, device_id_type=MESH)
    for j in range(1, chips):
        peer = xor(chip, j, chips) * 2 + core
        pl.semaphore_signal(barrier, inc=1, device_id={"freq": peer}, device_id_type=MESH)
    pl.semaphore_signal(barrier, inc=1, device_id={"freq": chip * 2 + other}, device_id_type=MESH)

    for load in loads[4:]:
        load.start()
    for load in loads[:2]:
        load.wait()

    def dom_copy(j, source, target, send, recv, sender):
        return pltpu.make_async_remote_copy(
            src_ref=source,
            dst_ref=target.at[sender],
            send_sem=send.at[j],
            recv_sem=recv.at[sender],
            device_id={"dom": xor(dom, j, doms)},
            device_id_type=MESH,
        )

    def v_copy(j, sender):
        return dom_copy(j, v_ref.at[:, :border], seen, v_send, v_recv, sender)

    def edge_copy(j, owner, sender):
        return dom_copy(j, edge_out(owner), edge, edge_send, edge_recv, sender)

    if stride > rank:
        for j in range(1, chips):
            gap = (code.shape[0], stride - rank, code.shape[2])
            code[:, j * stride - gap[1] : j * stride] = jnp.zeros(gap, jnp.float32)

    high, low = split(v_ref[...])
    volt[:rows, :nodes] = high
    volt[rows:, :nodes] = low

    def build(i, carry):
        @pl.when(i == 1)
        def _():
            pl.semaphore_wait(barrier, doms + chips - 1)
            for j in range(doms - 1, 0, -1):
                v_copy(j, dom).start()

        cols = pl.ds(pl.multiple_of(i * bw, bw), bw)
        first = term_ref[0:1, cols]
        second = term_ref[1:2, cols]
        same = first == second
        first = jnp.where(same, -1, first)
        second = jnp.where(same, -1, second)
        total = jnp.zeros((2 * rows, bw), jnp.float32)
        base = lax.broadcasted_iota(jnp.int16, (kb, bw), 0)
        for k in range(wide // kb):
            plus = base == (first - k * kb).astype(jnp.int16)
            minus = base == (second - k * kb).astype(jnp.int16)
            tile = jnp.where(plus, one, jnp.where(minus, -one, zero))
            inc[k * kb : (k + 1) * kb, cols] = tile
            if k * kb < nodes:
                total = total + dot(volt[:, k * kb : (k + 1) * kb], tile)
        partial[:, cols] = total[:rows] + total[rows:]
        return carry

    lax.fori_loop(0, elems // bw, build, 0)

    for load in loads[2:4]:
        load.wait()
    seen[dom] = v_ref[:, :border]
    for j in range(1, doms):
        v_copy(j, xor(dom, j, doms)).wait_recv()
    for p in range(doms):
        high, low = split(seen[p])
        volt[:rows, nodes + p * border : nodes + (p + 1) * border] = high
        volt[rows:, nodes + p * border : nodes + (p + 1) * border] = low

    def evaluate(i, carry):
        cols = pl.ds(pl.multiple_of(i * ew, ew), ew)
        total = dot(volt[:, nodes:], inc[nodes:, cols])
        across = partial[:, cols] + (total[:rows] + total[rows:])
        current = cur_ref[0:1, cols] * across + cur_ref[1:2, cols] * jnp.tanh(2.0 * across)
        charge = chg_ref[0:1, cols] * across + chg_ref[1:2, cols] * jnp.tanh(across)
        high, low = split(current)
        flow[:rows, cols] = high
        flow[rows : 2 * rows, cols] = low
        high, low = split(charge)
        flow[2 * rows : 3 * rows, cols] = high
        flow[3 * rows :, cols] = low
        return carry

    lax.fori_loop(0, elems // ew, evaluate, 0)

    blocks = half // border
    own = 2 * rows

    def scatter(*starts):
        rows_at = [inc[pl.ds(pl.multiple_of(s, border), border), :] for s in starts]
        total = dot(flow[...], jnp.concatenate(rows_at, axis=0), ((1,), (1,)))
        current = total[:rows] + total[rows : 2 * rows]
        charge = total[2 * rows : 3 * rows] + total[3 * rows :]
        return jnp.concatenate([current, charge], axis=0)

    def edge_out(owner):
        cols = pl.ds(pl.multiple_of(owner % 2 * border, border), border)
        return stage.at[blocks + owner // 2, :, cols]

    def rows_of(which):
        return pl.ds(pl.multiple_of(which * rows, rows), rows)

    def columns_of(which, b):
        return pl.ds(pl.multiple_of(which * half + b * border, border), border)

    def core_copy(b):
        return pltpu.make_async_remote_copy(
            src_ref=stage.at[b, :, :border],
            dst_ref=land.at[b],
            send_sem=core_send.at[b],
            recv_sem=core_recv.at[b],
            device_id={"freq": chip * 2 + other},
            device_id_type=MESH,
        )

    def code_copy(b, j):
        piece = pl.ds((j - 1) * stride, rank)
        return pltpu.make_async_remote_copy(
            src_ref=code_out.at[b, piece],
            dst_ref=code.at[b, piece],
            send_sem=code_send.at[b, j],
            recv_sem=code_recv.at[b, j],
            device_id={"freq": xor(chip, j, chips) * 2 + core},
            device_id_type=MESH,
        )

    def back_copy(b, sender):
        return pltpu.make_async_remote_copy(
            src_ref=coef.at[b, rows_of(other)],
            dst_ref=both_ref.at[0, :, columns_of(sender, b)],
            send_sem=back_send.at[b],
            recv_sem=back_recv.at[b],
            device_id={"freq": chip * 2 + other},
            device_id_type=MESH,
        )

    def product(high, low, x):
        x_high, x_low = split(x)
        return dot(high, x_high) + (dot(high, x_low) + dot(low, x_high))

    for load in loads[4:]:
        load.wait()

    far = sorted(range(1, chips), key=lambda j: -j)

    rims = doms // 2

    steps = blocks + rims

    def is_rim(i):
        return jnp.logical_and(i >= 1, i <= rims)

    def block_of(i):
        return blocks - 1 - jnp.where(i == 0, 0, i - rims)

    def node_block(i, carry):
        rim = is_rim(i)
        b = block_of(i)
        edge_at = nodes + 2 * (i - 1) * border

        @pl.when(i < steps)
        def _():
            there = jnp.where(rim, edge_at, other * half + b * border)
            here = jnp.where(rim, edge_at + border, core * half + b * border)
            stage[jnp.where(rim, blocks + i - 1, b)] = scatter(there, here)

        @pl.when(i == rims)
        def _():
            for k in range(doms - 1, 0, -1):
                edge_copy(k, xor(dom, k, doms), dom).start()

        @pl.when(i == steps - 1)
        def _():
            for k in range(1, doms):
                edge_copy(k, dom, xor(dom, k, doms)).wait_recv()
            cols = pl.ds(pl.multiple_of(other * border, border), border)
            total = stage[0, :, cols] + edge_out(dom)[...]
            for p in range(doms):
                total = total + jnp.where(dom == p, 0.0, edge[p])
            stage[0, :, cols] = total

        @pl.when(jnp.logical_and(i < steps, jnp.logical_not(rim)))
        def _():
            core_copy(b).start()

        @pl.when(jnp.logical_and(i >= 1, jnp.logical_not(is_rim(i - 1))))
        def _():
            done = block_of(i - 1)
            core_copy(done).wait_recv()
            flows = jnp.concatenate([stage[done, :, border:], land[done]], axis=0)
            result = product(eh_ref[...], el_ref[...], flows)
            coef[done] = result[:own]
            code_out[done] = result[own:]
            for j in far:
                code_copy(done, j).start()

        return carry

    lax.fori_loop(0, steps + 1, node_block, 0)

    def join(b):
        for j in far:
            code_copy(b, j).wait_recv()
        coef[b] = coef[b] + product(dh_ref[...], dl_ref[...], code[b])
        back_copy(b, core).start()
        both_ref[0, :, columns_of(core, b)] = coef[b, rows_of(core)]

    even = lax.broadcasted_iota(jnp.int32, (rows, LANES), 0) % 2 == 0

    def fold(x):
        return jnp.sum((x * x).reshape(rows // 8, 8, LANES), axis=0)

    def finish(b, sums):
        def piece(i, carry):
            @pl.when(i == 1)
            def _():
                back_copy(b, other).wait_recv()

            cols = columns_of(jnp.where(i == 1, other, core), b)
            residual = both_ref[0, :, cols] - src_ref[:, cols]
            upper = jnp.where(even, residual, pltpu.roll(residual, 1, 0))
            lower = jnp.where(even, pltpu.roll(residual, rows - 1, 0), residual)
            raw = -(jac_ref[:, 0, cols] * upper + jac_ref[:, 1, cols] * lower)
            both_ref[0, :, cols] = residual
            both_ref[1, :, cols] = raw
            return carry[0] + fold(raw), carry[1] + fold(residual)

        return lax.fori_loop(0, 2, piece, sums)

    zeros = jnp.zeros((8, LANES), jnp.float32)

    def close(i, sums):
        b = blocks - 1 - i
        join(b)
        return lax.cond(i > 0, lambda s: finish(b + 1, s), lambda s: s, sums)

    sums = finish(0, lax.fori_loop(0, blocks, close, (zeros, zeros)))

    def halves(x):
        return x + pltpu.roll(x, LANES // 2, 1)

    folded = jnp.where(
        lax.broadcasted_iota(jnp.int32, (8, LANES), 1) < LANES // 2, halves(sums[0]), halves(sums[1])
    )
    lane = lax.broadcasted_iota(jnp.int32, (1, LANES), 1)
    count = doms * freqs
    me = dom * freqs + freq
    part[me] = jnp.sum(folded, axis=0, keepdims=True)

    def part_copy(j, sending):
        dom_at, freq_at = xor(dom, j // freqs, doms), xor(freq, j % freqs, freqs)
        return pltpu.make_async_remote_copy(
            src_ref=part.at[me],
            dst_ref=part.at[me if sending else dom_at * freqs + freq_at],
            send_sem=part_send.at[j],
            recv_sem=part_recv.at[j],
            device_id={"dom": dom_at, "freq": freq_at},
            device_id_type=MESH,
        )

    for j in range(count - 1, 0, -1):
        part_copy(j, True).start()
    for j in range(count - 1, 0, -1):
        part_copy(j, False).wait_recv()
    total = jnp.sum(part[...], axis=0)
    raw_sum = jnp.sum(jnp.where(lane < LANES // 2, total, 0.0), axis=1, keepdims=True)
    res_sum = jnp.sum(jnp.where(lane < LANES // 2, 0.0, total), axis=1, keepdims=True)
    spread = jnp.sqrt(raw_sum / entries + 1e-06)
    both_ref[1] = both_ref[1] * jnp.minimum(1.0, trust_radius / spread)
    norm_ref[...] = jnp.sqrt(res_sum)

    for j in range(1, doms):
        v_copy(j, dom).wait_send()
        edge_copy(j, dom, dom).wait_send()

    for b in range(blocks):
        core_copy(b).wait_send()
        back_copy(b, core).wait_send()
        for j in far:
            code_copy(b, j).wait_send()

    for j in range(1, count):
        part_copy(j, True).wait_send()


def place_kernel(both_any, norm_any, residual_any, step_any, out_norm_any, sem):
    copies = [
        pltpu.make_async_copy(a, b, sem.at[i])
        for i, (a, b) in enumerate(
            ((both_any.at[0], residual_any), (both_any.at[1], step_any), (norm_any, out_norm_any))
        )
    ]
    for copy in copies:
        copy.start()
    for copy in copies:
        copy.wait()


def body(doms, freqs, voltages, sources, terminals, elem_current, elem_charge, jacobi):
    rows, nodes = voltages.shape
    elems = terminals.shape[1]
    border = nodes // 16
    wide = nodes + doms * border
    samples = rows * freqs
    chips = freqs // 2
    blocks = nodes // 2 // border
    own = 2 * rows
    f32, bf16 = jnp.float32, jnp.bfloat16
    dma = pltpu.SemaphoreType.DMA
    vmem = pl.BlockSpec(memory_space=VMEM)
    anywhere = pl.BlockSpec(memory_space=pl.ANY)
    encode, decode, rank, stride = exchange_tables(samples, chips)
    codes = (chips - 1) * stride
    both, norm = pl.pallas_call(
        functools.partial(kernel, doms, freqs, float(samples * nodes * doms), rank, stride),
        out_shape=(
            VMEM((2, rows, nodes), f32),
            jax.ShapeDtypeStruct((1, 1), f32),
        ),
        in_specs=[anywhere] * 10,
        out_specs=(vmem, vmem),
        scratch_shapes=[
            VMEM((2 * rows, wide), bf16),
            VMEM((doms, rows, border), f32),
            VMEM((wide, elems), bf16),
            VMEM((rows, elems), f32),
            VMEM((4 * rows, elems), bf16),
            VMEM((blocks + doms // 2, own, 2 * border), f32),
            VMEM((blocks, own, border), f32),
            VMEM((doms, own, border), f32),
            VMEM((blocks, own, border), f32),
            VMEM((blocks, codes, border), f32),
            VMEM((blocks, codes, border), f32),
            VMEM((rows, nodes), f32),
            VMEM((2, elems), jnp.int32),
            VMEM((2, elems), f32),
            VMEM((2, elems), f32),
            VMEM((rows, nodes), f32),
            VMEM((rows, 2, nodes), f32),
            VMEM((own + codes, 2 * own), bf16),
            VMEM((own + codes, 2 * own), bf16),
            VMEM((own, codes), bf16),
            VMEM((own, codes), bf16),
            VMEM((doms * freqs, 1, LANES), f32),
            dma((doms,)), dma((doms,)),
            dma((doms,)), dma((doms,)),
            dma((blocks,)), dma((blocks,)),
            dma((blocks, chips)), dma((blocks, chips)),
            dma((blocks,)), dma((blocks,)),
            dma((doms * freqs,)), dma((doms * freqs,)),
            dma((10,)),
        ],
        compiler_params=pltpu.CompilerParams(
            collective_id=0, has_side_effects=True, vmem_limit_bytes=56 * 1024 * 1024
        ),
    )(
        voltages, terminals, elem_current, elem_charge,
        sources, jacobi.reshape(rows, 2, nodes), *map(jnp.asarray, encode + decode),
    )
    residual, step, norm = pl.pallas_call(
        place_kernel,
        out_shape=(
            jax.ShapeDtypeStruct((rows, nodes), f32),
            jax.ShapeDtypeStruct((rows, nodes), f32),
            jax.ShapeDtypeStruct((1, 1), f32),
        ),
        in_specs=[anywhere] * 2,
        out_specs=(anywhere,) * 3,
        scratch_shapes=[dma((3,))],
        compiler_params=pltpu.CompilerParams(vmem_limit_bytes=1024 * 1024),
    )(both, norm)
    return residual, step, norm.reshape(())


def solution(mesh):
    placed = (
        P("freq", "dom"),
        P("freq", "dom"),
        P(None, "dom"),
        P(None, "dom"),
        P(None, "dom"),
        P("freq", None, None, "dom"),
    )
    return jax.shard_map(
        functools.partial(body, mesh.shape["dom"], mesh.shape["freq"]),
        mesh=mesh,
        in_specs=placed,
        out_specs=(P("freq", "dom"), P("freq", "dom"), P()),
        check_vma=False,
    )
```

```python
import functools
import math

import jax
import jax.numpy as jnp
import numpy as np
from jax import lax
from jax.experimental import pallas as pl
from jax.experimental.pallas import tpu as pltpu
from jax.sharding import PartitionSpec as P

MESH = pl.DeviceIdType.MESH
LANES = 128
VMEM = pltpu.VMEM
trust_radius = 2.0
TOLERANCE = 6e-7
DIRECT = 2


def fourier_tables(samples):
    row = np.arange(samples)
    harmonic = row // 2
    sine = row % 2 == 1
    order = np.where(harmonic == 0, np.where(sine, samples // 2, 0), harmonic)
    phase = (order[:, None] * np.arange(samples)[None, :] % samples) * (2.0 * math.pi / samples)
    values = np.where((sine & (harmonic > 0))[:, None], np.sin(phase), np.cos(phase))
    weight = np.where(harmonic == 0, math.sqrt(1.0 / samples), math.sqrt(2.0 / samples))
    full = values * weight[:, None]
    pairs = full.reshape(samples // 2, 2, samples)
    rate = (2.0 / samples) * np.arange(samples // 2)
    derived = np.stack([pairs[:, 1], -pairs[:, 0]], axis=1) * rate[:, None, None]
    return full, derived.reshape(samples, samples)


def split_table(full):
    full = full.astype(np.float32)
    high = full.astype(jnp.bfloat16)
    low = (full - high.astype(np.float32)).astype(jnp.bfloat16)
    return high, low


def up(value, step):
    return -(-value // step) * step


def exchange_tables(samples, chips):
    full, derived = fourier_tables(samples)
    own = samples // chips
    part = own // 2
    blocks, rank = {}, 0
    for k in range(chips):
        for m in range(chips):
            rows, first, second = slice(m * own, (m + 1) * own), k * own, k * own + part
            block = np.concatenate(
                [t[rows, s : s + part] for s in (first, second) for t in (full, derived)], axis=1
            )
            blocks[m, k] = block
            if m != k:
                values = np.linalg.svd(block, compute_uv=False)
                rank = max(rank, int((values > TOLERANCE * values[0]).sum()))
    rank = up(rank, 8)
    stride = up(rank, 16)
    encode = np.zeros((chips, 2, own + (chips - 1) * stride, 2 * own))
    decode = np.zeros((chips, own, (chips - 1) * stride))
    for k in range(chips):
        encode[k, :, :own] = blocks[k, k]
        for j in range(1, chips):
            start = (j - 1) * stride
            left, values, right = np.linalg.svd(blocks[k ^ j, k], full_matrices=False)
            encode[k, :, own + start : own + start + rank] = values[:rank, None] * right[:rank]
            decode[k ^ j, :, start : start + rank] = left[:, :rank]
    relayed = relay_tables(blocks, encode, decode, rank, stride) if chips == 4 else None
    tables = [per_core(encode)[:, None], decode[:, None], np.zeros((chips, 16, LANES))]
    if relayed is not None:
        enc, dec, add = relayed[0]
        tables = [both_modes(per_core(encode), enc, 1), both_modes(decode, dec, 2), add]
    flat = [half for table in tables for half in split_table(table)]
    return flat, rank, stride, relayed[1:] if relayed is not None else None


def per_core(encode):
    own = encode.shape[3] // 2
    encode = encode.copy()
    encode[:, 1] = np.roll(encode[:, 1], own, axis=2)
    return encode.reshape((-1,) + encode.shape[2:])


def both_modes(first, second, axis):
    size = max(first.shape[axis], second.shape[axis])
    pads = [[(0, size - t.shape[i] if i == axis else 0) for i in range(3)] for t in (first, second)]
    return np.stack([np.pad(first, pads[0]), np.pad(second, pads[1])], axis=1)


def factor(block):
    left, values, right = np.linalg.svd(block, full_matrices=False)
    return left, values[:, None] * right, int((values > TOLERANCE * values[0]).sum())


def relay_tables(blocks, encode, decode, rank, stride):
    own = decode.shape[1]
    lines = ((0, 1, 2, 3), (3, 2, 1, 0))
    joint, merged = {}, {}
    for outer, inner, *far in lines:
        joint[inner] = factor(np.concatenate([blocks[d, outer] for d in far], axis=0))
        for d in far:
            merged[d] = factor(np.concatenate([blocks[d, inner], blocks[d, outer]], axis=1))
    joint_rank = up(max(j[2] for j in joint.values()), 8)
    merged_rank = up(max(m[2] for m in merged.values()), 8)
    width = up(max(joint_rank, merged_rank), 16)
    enc = np.zeros((4, 2, own + stride + 2 * width, 2 * own))
    dec = np.zeros((4, own, stride + width))
    add = np.zeros((4, 2 * width, width))
    enc[:, :, : own + stride] = encode[:, :, : own + stride]
    dec[:, :, :stride] = decode[:, :, :stride]
    start = own + stride
    for outer, inner, *far in lines:
        left, right, _ = joint[inner]
        enc[outer, :, start : start + joint_rank] = right[:joint_rank]
        for i, d in enumerate(far):
            basis = merged[d][0][:, :merged_rank]
            rows = slice(i * width, i * width + merged_rank)
            enc[inner, :, start + rows.start : start + rows.stop] = basis.T @ blocks[d, inner]
            add[inner, rows, :joint_rank] = basis.T @ left[i * own : (i + 1) * own, :joint_rank]
            dec[d, :, stride : stride + merged_rank] = basis
    return [per_core(enc), dec, add], joint_rank, merged_rank, width


def split(x):
    high = x.astype(jnp.bfloat16)
    low = (x - high.astype(jnp.float32)).astype(jnp.bfloat16)
    return high, low


def dot(a, b, contract=((1,), (0,))):
    return lax.dot_general(a, b, (contract, ((), ())), preferred_element_type=jnp.float32)


def xor(a, b, count):
    out, bit = 0, 1
    while bit < count:
        out = out + bit * ((a // bit + b // bit) % 2)
        bit *= 2
    return out


def kernel(
    doms, freqs, entries, rank, stride, relay,
    v_any, term_any, cur_any, chg_any, src_any, jac_any,
    eh_any, el_any, dh_any, dl_any, ah_any, al_any,
    both_ref, norm_ref,
    volt, seen, inc, partial, flow, stage, land, edge, coef, code_out, code, joint,
    v_ref, term_ref, cur_ref, chg_ref, src_ref, jac_ref, eh_ref, el_ref, dh_ref, dl_ref, ah_ref, al_ref, part,
    v_send, v_recv, edge_send, edge_recv, core_send, core_recv, code_send, code_recv, back_send, back_recv,
    part_send, part_recv, load_sem,
):
    dom = lax.axis_index("dom")
    freq = lax.axis_index("freq")
    rows, nodes = v_ref.shape
    wide, elems = inc.shape
    border = seen.shape[2]
    chips = freqs // 2
    chip = freq // 2
    core = freq % 2
    other = 1 - core
    half = nodes // 2
    bw = min(2048, elems)
    ew = min(2048, elems)
    kb = 256
    one, zero = jnp.bfloat16(1.0), jnp.bfloat16(0.0)

    loads = [
        pltpu.make_async_copy(a, b, load_sem.at[i])
        for i, (a, b) in enumerate(
            (
                (term_any, term_ref), (v_any, v_ref), (cur_any, cur_ref), (chg_any, chg_ref),
                (eh_any.at[freq], eh_ref), (el_any.at[freq], el_ref),
                (dh_any.at[chip], dh_ref), (dl_any.at[chip], dl_ref),
                (ah_any.at[chip], ah_ref), (al_any.at[chip], al_ref),
                (src_any, src_ref), (jac_any, jac_ref),
            )
        )
    ]
    for load in loads[:4]:
        load.start()

    barrier = pltpu.get_barrier_semaphore()
    for j in range(1, doms):
        pl.semaphore_signal(barrier, inc=1, device_id={"dom": xor(dom, j, doms)}, device_id_type=MESH)
    for j in range(1, chips):
        peer = xor(chip, j, chips) * 2 + core
        pl.semaphore_signal(barrier, inc=1, device_id={"freq": peer}, device_id_type=MESH)
    pl.semaphore_signal(barrier, inc=1, device_id={"freq": chip * 2 + other}, device_id_type=MESH)

    for load in loads[4:]:
        load.start()
    for load in loads[:2]:
        load.wait()

    def dom_copy(j, source, target, send, recv, sender):
        return pltpu.make_async_remote_copy(
            src_ref=source,
            dst_ref=target.at[sender],
            send_sem=send.at[j],
            recv_sem=recv.at[sender],
            device_id={"dom": xor(dom, j, doms)},
            device_id_type=MESH,
        )

    def v_copy(j, sender):
        return dom_copy(j, v_ref.at[:, :border], seen, v_send, v_recv, sender)

    def edge_copy(j, owner, sender):
        return dom_copy(j, edge_out(owner), edge, edge_send, edge_recv, sender)

    blocks = half // border
    direct = min(DIRECT, blocks) if relay else blocks
    inner = chip % 4 % 3 != 0
    if relay:
        joint_rank, merged_rank, width = relay

    def clear(ref, b, start, stop):
        if stop > start:
            ref[b, start:stop] = jnp.zeros((stop - start, border), jnp.float32)

    for b in range(blocks):
        clear(code, b, rank, stride)
        if b >= blocks - direct:
            for j in range(2, chips):
                clear(code, b, j * stride - stride + rank, j * stride)
            clear(code, b, (chips - 1) * stride, code.shape[1])
        else:
            clear(code, b, stride + merged_rank, code.shape[1])
            clear(joint, b, joint_rank, width)

    high, low = split(v_ref[...])
    volt[:rows, :nodes] = high
    volt[rows:, :nodes] = low

    def build(i, carry):
        @pl.when(i == 1)
        def _():
            pl.semaphore_wait(barrier, doms + chips - 1)
            for j in range(doms - 1, 0, -1):
                v_copy(j, dom).start()

        cols = pl.ds(pl.multiple_of(i * bw, bw), bw)
        first = term_ref[0:1, cols]
        second = term_ref[1:2, cols]
        same = first == second
        first = jnp.where(same, -1, first)
        second = jnp.where(same, -1, second)
        total = jnp.zeros((2 * rows, bw), jnp.float32)
        base = lax.broadcasted_iota(jnp.int16, (kb, bw), 0)
        for k in range(wide // kb):
            plus = base == (first - k * kb).astype(jnp.int16)
            minus = base == (second - k * kb).astype(jnp.int16)
            tile = jnp.where(plus, one, jnp.where(minus, -one, zero))
            inc[k * kb : (k + 1) * kb, cols] = tile
            if k * kb < nodes:
                total = total + dot(volt[:, k * kb : (k + 1) * kb], tile)
        partial[:, cols] = total[:rows] + total[rows:]
        return carry

    lax.fori_loop(0, elems // bw, build, 0)

    for load in loads[2:4]:
        load.wait()
    seen[dom] = v_ref[:, :border]
    for j in range(1, doms):
        v_copy(j, xor(dom, j, doms)).wait_recv()
    for p in range(doms):
        high, low = split(seen[p])
        volt[:rows, nodes + p * border : nodes + (p + 1) * border] = high
        volt[rows:, nodes + p * border : nodes + (p + 1) * border] = low

    def evaluate(i, carry):
        cols = pl.ds(pl.multiple_of(i * ew, ew), ew)
        total = dot(volt[:, nodes:], inc[nodes:, cols])
        across = partial[:, cols] + (total[:rows] + total[rows:])
        current = cur_ref[0:1, cols] * across + cur_ref[1:2, cols] * jnp.tanh(2.0 * across)
        charge = chg_ref[0:1, cols] * across + chg_ref[1:2, cols] * jnp.tanh(across)
        high, low = split(current)
        flow[:rows, cols] = high
        flow[rows : 2 * rows, cols] = low
        high, low = split(charge)
        flow[2 * rows : 3 * rows, cols] = high
        flow[3 * rows :, cols] = low
        return carry

    lax.fori_loop(0, elems // ew, evaluate, 0)

    own = 2 * rows

    def scatter(*starts):
        rows_at = [inc[pl.ds(pl.multiple_of(s, border), border), :] for s in starts]
        total = dot(flow[...], jnp.concatenate(rows_at, axis=0), ((1,), (1,)))
        current = total[:rows] + total[rows : 2 * rows]
        charge = total[2 * rows : 3 * rows] + total[3 * rows :]
        return jnp.concatenate([current, charge], axis=0)

    def edge_out(owner):
        cols = pl.ds(pl.multiple_of(owner % 2 * border, border), border)
        return stage.at[blocks + owner // 2, :, cols]

    def rows_of(which):
        return pl.ds(pl.multiple_of(which * rows, rows), rows)

    def columns_of(which, b):
        return pl.ds(pl.multiple_of(which * half + b * border, border), border)

    def core_copy(b):
        return pltpu.make_async_remote_copy(
            src_ref=stage.at[b, :, :border],
            dst_ref=land.at[b],
            send_sem=core_send.at[b],
            recv_sem=core_recv.at[b],
            device_id={"freq": chip * 2 + other},
            device_id_type=MESH,
        )

    def code_copy(b, j):
        piece = pl.ds((j - 1) * stride, rank)
        return pltpu.make_async_remote_copy(
            src_ref=code_out.at[b, piece],
            dst_ref=code.at[b, piece],
            send_sem=code_send.at[b, j],
            recv_sem=code_recv.at[b, j],
            device_id={"freq": xor(chip, j, chips) * 2 + core},
            device_id_type=MESH,
        )

    def send(b, source, target, count, send_at, recv_at, j):
        return pltpu.make_async_remote_copy(
            src_ref=code_out.at[b, pl.ds(source, count)],
            dst_ref=target,
            send_sem=code_send.at[b, send_at],
            recv_sem=code_recv.at[b, recv_at],
            device_id={"freq": xor(chip, j, chips) * 2 + core},
            device_id_type=MESH,
        )

    def joint_copy(b):
        return send(b, stride, joint.at[b, pl.ds(0, joint_rank)], joint_rank, 2, 3, 1)

    def merged_copy(b, i):
        target = code.at[b, pl.ds(stride, merged_rank)]
        return send(b, stride + i * width, target, merged_rank, 2 + i, 2, 3 - i)

    def back_copy(b, sender):
        return pltpu.make_async_remote_copy(
            src_ref=coef.at[b, rows_of(other)],
            dst_ref=both_ref.at[0, :, columns_of(sender, b)],
            send_sem=back_send.at[b],
            recv_sem=back_recv.at[b],
            device_id={"freq": chip * 2 + other},
            device_id_type=MESH,
        )

    def product(high, low, x):
        x_high, x_low = split(x)
        return dot(high, x_high) + (dot(high, x_low) + dot(low, x_high))

    for load in loads[4:]:
        load.wait()

    far = sorted(range(1, chips), key=lambda j: -j)

    rims = doms // 2

    steps = blocks + rims
    ahead = blocks // 2 + 1

    lag = 3

    def is_block(i):
        return jnp.logical_and(jnp.logical_and(i >= 0, i < steps), jnp.logical_not(is_rim(i)))

    def is_rim(i):
        return jnp.logical_and(i >= ahead, i < ahead + rims)

    def block_of(i):
        return blocks - 1 - jnp.where(i < ahead, i, i - rims)

    def node_block(i, carry):
        rim = is_rim(i)
        b = block_of(i)
        edge_at = nodes + 2 * (i - ahead) * border

        @pl.when(i < steps)
        def _():
            there = jnp.where(rim, edge_at, other * half + b * border)
            here = jnp.where(rim, edge_at + border, core * half + b * border)
            stage[jnp.where(rim, blocks + i - ahead, b)] = scatter(there, here)

        @pl.when(i == ahead + rims - 1)
        def _():
            for k in range(doms - 1, 0, -1):
                edge_copy(k, xor(dom, k, doms), dom).start()

        @pl.when(i == steps - 1)
        def _():
            for k in range(1, doms):
                edge_copy(k, dom, xor(dom, k, doms)).wait_recv()
            cols = pl.ds(pl.multiple_of(other * border, border), border)
            total = stage[0, :, cols] + edge_out(dom)[...]
            for p in range(doms):
                total = total + jnp.where(dom == p, 0.0, edge[p])
            stage[0, :, cols] = total

        @pl.when(jnp.logical_and(i < steps, jnp.logical_not(rim)))
        def _():
            core_copy(b).start()

        done = block_of(i - 1)
        straight = done >= blocks - direct

        def flows():
            return jnp.concatenate([stage[done, :, border:], land[done]], axis=0)

        @pl.when(is_block(i - 1))
        def _():
            core_copy(done).wait_recv()
            mode = jnp.where(straight, 0, 1)
            result = product(eh_ref[mode], el_ref[mode], flows())
            coef[done] = result[:own]
            code_out[done] = result[own:]

            @pl.when(straight)
            def _():
                for j in far[:-1]:
                    code_copy(done, j).start()

            if direct < blocks:
                @pl.when(jnp.logical_not(jnp.logical_or(straight, inner)))
                def _():
                    joint_copy(done).start()

        if direct < blocks:
            old = block_of(i - 1 - lag)
            late = jnp.logical_and(is_block(i - 1 - lag), old < blocks - direct)

            @pl.when(jnp.logical_and(late, inner))
            def _():
                joint_copy(old).wait_recv()
                both = pl.ds(stride, 2 * width)
                code_out[old, both] = code_out[old, both] + product(ah_ref[...], al_ref[...], joint[old])
                for k in range(2):
                    merged_copy(old, k).start()

        @pl.when(is_block(i - 1 - lag))
        def _():
            code_copy(block_of(i - 1 - lag), 1).start()

        return carry

    lax.fori_loop(0, steps + 1 + lag, node_block, 0)

    def join(b):
        code_copy(b, 1).wait_recv()

        straight = b >= blocks - direct

        @pl.when(straight)
        def _():
            for j in far[:-1]:
                code_copy(b, j).wait_recv()

        if direct < blocks:
            @pl.when(jnp.logical_not(straight))
            def _():
                merged_copy(b, 0).wait_recv()

        mode = jnp.where(straight, 0, 1)
        coef[b] = coef[b] + product(dh_ref[mode], dl_ref[mode], code[b])
        back_copy(b, core).start()
        both_ref[0, :, columns_of(core, b)] = coef[b, rows_of(core)]

    even = lax.broadcasted_iota(jnp.int32, (rows, LANES), 0) % 2 == 0

    def fold(x):
        return jnp.sum((x * x).reshape(rows // 8, 8, LANES), axis=0)

    def finish(b, sums):
        def piece(i, carry):
            @pl.when(i == 1)
            def _():
                back_copy(b, other).wait_recv()

            cols = columns_of(jnp.where(i == 1, other, core), b)
            residual = both_ref[0, :, cols] - src_ref[:, cols]
            upper = jnp.where(even, residual, pltpu.roll(residual, 1, 0))
            lower = jnp.where(even, pltpu.roll(residual, rows - 1, 0), residual)
            raw = -(jac_ref[:, 0, cols] * upper + jac_ref[:, 1, cols] * lower)
            both_ref[0, :, cols] = residual
            both_ref[1, :, cols] = raw
            return carry[0] + fold(raw), carry[1] + fold(residual)

        return lax.fori_loop(0, 2, piece, sums)

    zeros = jnp.zeros((8, LANES), jnp.float32)

    def close(i, sums):
        b = blocks - 1 - i
        join(b)
        return lax.cond(i > 0, lambda s: finish(b + 1, s), lambda s: s, sums)

    sums = finish(0, lax.fori_loop(0, blocks, close, (zeros, zeros)))

    def halves(x):
        return x + pltpu.roll(x, LANES // 2, 1)

    folded = jnp.where(
        lax.broadcasted_iota(jnp.int32, (8, LANES), 1) < LANES // 2, halves(sums[0]), halves(sums[1])
    )
    lane = lax.broadcasted_iota(jnp.int32, (1, LANES), 1)
    count = doms * freqs
    me = dom * freqs + freq
    part[me] = jnp.sum(folded, axis=0, keepdims=True)

    def part_copy(j, sending):
        dom_at, freq_at = xor(dom, j // freqs, doms), xor(freq, j % freqs, freqs)
        return pltpu.make_async_remote_copy(
            src_ref=part.at[me],
            dst_ref=part.at[me if sending else dom_at * freqs + freq_at],
            send_sem=part_send.at[j],
            recv_sem=part_recv.at[j],
            device_id={"dom": dom_at, "freq": freq_at},
            device_id_type=MESH,
        )

    for j in range(count - 1, 0, -1):
        part_copy(j, True).start()
    for j in range(count - 1, 0, -1):
        part_copy(j, False).wait_recv()
    total = jnp.sum(part[...], axis=0)
    raw_sum = jnp.sum(jnp.where(lane < LANES // 2, total, 0.0), axis=1, keepdims=True)
    res_sum = jnp.sum(jnp.where(lane < LANES // 2, 0.0, total), axis=1, keepdims=True)
    spread = jnp.sqrt(raw_sum / entries + 1e-06)
    both_ref[1] = both_ref[1] * jnp.minimum(1.0, trust_radius / spread)
    norm_ref[...] = jnp.sqrt(res_sum)

    for j in range(1, doms):
        v_copy(j, dom).wait_send()
        edge_copy(j, dom, dom).wait_send()

    for b in range(blocks):
        core_copy(b).wait_send()
        back_copy(b, core).wait_send()
        code_copy(b, 1).wait_send()
        if b >= blocks - direct:
            for j in far[:-1]:
                code_copy(b, j).wait_send()
        else:
            @pl.when(inner)
            def _():
                for k in range(2):
                    merged_copy(b, k).wait_send()

            @pl.when(jnp.logical_not(inner))
            def _():
                joint_copy(b).wait_send()

    for j in range(1, count):
        part_copy(j, True).wait_send()


def place_kernel(both_any, norm_any, residual_any, step_any, out_norm_any, sem):
    copies = [
        pltpu.make_async_copy(a, b, sem.at[i])
        for i, (a, b) in enumerate(
            ((both_any.at[0], residual_any), (both_any.at[1], step_any), (norm_any, out_norm_any))
        )
    ]
    for copy in copies:
        copy.start()
    for copy in copies:
        copy.wait()


def body(doms, freqs, voltages, sources, terminals, elem_current, elem_charge, jacobi):
    rows, nodes = voltages.shape
    elems = terminals.shape[1]
    border = nodes // 16
    wide = nodes + doms * border
    samples = rows * freqs
    chips = freqs // 2
    blocks = nodes // 2 // border
    own = 2 * rows
    f32, bf16 = jnp.float32, jnp.bfloat16
    dma = pltpu.SemaphoreType.DMA
    vmem = pl.BlockSpec(memory_space=VMEM)
    anywhere = pl.BlockSpec(memory_space=pl.ANY)
    tables, rank, stride, relay = exchange_tables(samples, chips)
    codes = (chips - 1) * stride
    width = relay[2] if relay else 16
    both, norm = pl.pallas_call(
        functools.partial(kernel, doms, freqs, float(samples * nodes * doms), rank, stride, relay),
        out_shape=(
            VMEM((2, rows, nodes), f32),
            jax.ShapeDtypeStruct((1, 1), f32),
        ),
        in_specs=[anywhere] * 12,
        out_specs=(vmem, vmem),
        scratch_shapes=[
            VMEM((2 * rows, wide), bf16),
            VMEM((doms, rows, border), f32),
            VMEM((wide, elems), bf16),
            VMEM((rows, elems), f32),
            VMEM((4 * rows, elems), bf16),
            VMEM((blocks + doms // 2, own, 2 * border), f32),
            VMEM((blocks, own, border), f32),
            VMEM((doms, own, border), f32),
            VMEM((blocks, own, border), f32),
            VMEM((blocks, max(codes, stride + 2 * width) if relay else codes, border), f32),
            VMEM((blocks, max(codes, stride + width) if relay else codes, border), f32),
            VMEM((blocks, width, border), f32),
            VMEM((rows, nodes), f32),
            VMEM((2, elems), jnp.int32),
            VMEM((2, elems), f32),
            VMEM((2, elems), f32),
            VMEM((rows, nodes), f32),
            VMEM((rows, 2, nodes), f32),
            *(VMEM(table.shape[1:], bf16) for table in tables),
            VMEM((doms * freqs, 1, LANES), f32),
            dma((doms,)), dma((doms,)),
            dma((doms,)), dma((doms,)),
            dma((blocks,)), dma((blocks,)),
            dma((blocks, chips)), dma((blocks, chips)),
            dma((blocks,)), dma((blocks,)),
            dma((doms * freqs,)), dma((doms * freqs,)),
            dma((12,)),
        ],
        compiler_params=pltpu.CompilerParams(
            collective_id=0, has_side_effects=True, vmem_limit_bytes=56 * 1024 * 1024
        ),
    )(
        voltages, terminals, elem_current, elem_charge,
        sources, jacobi.reshape(rows, 2, nodes), *map(jnp.asarray, tables),
    )
    residual, step, norm = pl.pallas_call(
        place_kernel,
        out_shape=(
            jax.ShapeDtypeStruct((rows, nodes), f32),
            jax.ShapeDtypeStruct((rows, nodes), f32),
            jax.ShapeDtypeStruct((1, 1), f32),
        ),
        in_specs=[anywhere] * 2,
        out_specs=(anywhere,) * 3,
        scratch_shapes=[dma((3,))],
        compiler_params=pltpu.CompilerParams(vmem_limit_bytes=1024 * 1024),
    )(both, norm)
    return residual, step, norm.reshape(())


def solution(mesh):
    placed = (
        P("freq", "dom"),
        P("freq", "dom"),
        P(None, "dom"),
        P(None, "dom"),
        P(None, "dom"),
        P("freq", None, None, "dom"),
    )
    return jax.shard_map(
        functools.partial(body, mesh.shape["dom"], mesh.shape["freq"]),
        mesh=mesh,
        in_specs=placed,
        out_specs=(P("freq", "dom"), P("freq", "dom"), P()),
        check_vma=False,
    )
```

```python
import functools
import math

import jax
import jax.numpy as jnp
import numpy as np
from jax import lax
from jax.experimental import pallas as pl
from jax.experimental.pallas import tpu as pltpu
from jax.sharding import PartitionSpec as P

MESH = pl.DeviceIdType.MESH
LANES = 128
VMEM = pltpu.VMEM
trust_radius = 2.0
TOLERANCE = 6e-7
DIRECT = 2


def fourier_tables(samples):
    row = np.arange(samples)
    harmonic = row // 2
    sine = row % 2 == 1
    order = np.where(harmonic == 0, np.where(sine, samples // 2, 0), harmonic)
    phase = (order[:, None] * np.arange(samples)[None, :] % samples) * (2.0 * math.pi / samples)
    values = np.where((sine & (harmonic > 0))[:, None], np.sin(phase), np.cos(phase))
    weight = np.where(harmonic == 0, math.sqrt(1.0 / samples), math.sqrt(2.0 / samples))
    full = values * weight[:, None]
    pairs = full.reshape(samples // 2, 2, samples)
    rate = (2.0 / samples) * np.arange(samples // 2)
    derived = np.stack([pairs[:, 1], -pairs[:, 0]], axis=1) * rate[:, None, None]
    return full, derived.reshape(samples, samples)


def split_table(full):
    full = full.astype(np.float32)
    high = full.astype(jnp.bfloat16)
    low = (full - high.astype(np.float32)).astype(jnp.bfloat16)
    return np.concatenate([high, high, low], axis=-1)


def up(value, step):
    return -(-value // step) * step


def exchange_tables(samples, chips):
    full, derived = fourier_tables(samples)
    own = samples // chips
    part = own // 2
    blocks, rank = {}, 0
    for k in range(chips):
        for m in range(chips):
            rows, first, second = slice(m * own, (m + 1) * own), k * own, k * own + part
            block = np.concatenate(
                [t[rows, s : s + part] for s in (first, second) for t in (full, derived)], axis=1
            )
            blocks[m, k] = block
            if m != k:
                values = np.linalg.svd(block, compute_uv=False)
                rank = max(rank, int((values > TOLERANCE * values[0]).sum()))
    rank = up(rank, 8)
    stride = up(rank, 16)
    encode = np.zeros((chips, 2, own + (chips - 1) * stride, 2 * own))
    decode = np.zeros((chips, own, (chips - 1) * stride))
    for k in range(chips):
        encode[k, :, :own] = blocks[k, k]
        for j in range(1, chips):
            start = (j - 1) * stride
            left, values, right = np.linalg.svd(blocks[k ^ j, k], full_matrices=False)
            encode[k, :, own + start : own + start + rank] = values[:rank, None] * right[:rank]
            decode[k ^ j, :, start : start + rank] = left[:, :rank]
    relayed = relay_tables(blocks, encode, decode, rank, stride) if chips == 4 else None
    tables = [per_core(encode)[:, None], decode[:, None], np.zeros((chips, 16, LANES))]
    if relayed is not None:
        enc, dec, add = relayed[0]
        tables = [both_modes(per_core(encode), enc, 1), both_modes(decode, dec, 2), add]
    flat = [split_table(table) for table in tables]
    return flat, rank, stride, relayed[1:] if relayed is not None else None


def per_core(encode):
    own = encode.shape[3] // 2
    encode = encode.copy()
    encode[:, 1] = np.roll(encode[:, 1], own, axis=2)
    return encode.reshape((-1,) + encode.shape[2:])


def both_modes(first, second, axis):
    size = max(first.shape[axis], second.shape[axis])
    pads = [[(0, size - t.shape[i] if i == axis else 0) for i in range(3)] for t in (first, second)]
    return np.stack([np.pad(first, pads[0]), np.pad(second, pads[1])], axis=1)


def factor(block):
    left, values, right = np.linalg.svd(block, full_matrices=False)
    return left, values[:, None] * right, int((values > TOLERANCE * values[0]).sum())


def relay_tables(blocks, encode, decode, rank, stride):
    own = decode.shape[1]
    lines = ((0, 1, 2, 3), (3, 2, 1, 0))
    joint, merged = {}, {}
    for outer, inner, *far in lines:
        joint[inner] = factor(np.concatenate([blocks[d, outer] for d in far], axis=0))
        for d in far:
            merged[d] = factor(np.concatenate([blocks[d, inner], blocks[d, outer]], axis=1))
    joint_rank = up(max(j[2] for j in joint.values()), 8)
    merged_rank = up(max(m[2] for m in merged.values()), 8)
    width = up(max(joint_rank, merged_rank), 16)
    enc = np.zeros((4, 2, own + stride + 2 * width, 2 * own))
    dec = np.zeros((4, own, stride + width))
    add = np.zeros((4, 2 * width, width))
    enc[:, :, : own + stride] = encode[:, :, : own + stride]
    dec[:, :, :stride] = decode[:, :, :stride]
    start = own + stride
    for outer, inner, *far in lines:
        left, right, _ = joint[inner]
        enc[outer, :, start : start + joint_rank] = right[:joint_rank]
        for i, d in enumerate(far):
            basis = merged[d][0][:, :merged_rank]
            rows = slice(i * width, i * width + merged_rank)
            enc[inner, :, start + rows.start : start + rows.stop] = basis.T @ blocks[d, inner]
            add[inner, rows, :joint_rank] = basis.T @ left[i * own : (i + 1) * own, :joint_rank]
            dec[d, :, stride : stride + merged_rank] = basis
    return [per_core(enc), dec, add], joint_rank, merged_rank, width


def split(x):
    high = x.astype(jnp.bfloat16)
    low = (x - high.astype(jnp.float32)).astype(jnp.bfloat16)
    return high, low


def dot(a, b, contract=((1,), (0,))):
    return lax.dot_general(a, b, (contract, ((), ())), preferred_element_type=jnp.float32)


def xor(a, b, count):
    out, bit = 0, 1
    while bit < count:
        out = out + bit * ((a // bit + b // bit) % 2)
        bit *= 2
    return out


def kernel(
    doms, freqs, entries, rank, stride, relay,
    v_any, term_any, cur_any, chg_any, src_any, jac_any,
    enc_any, dec_any, add_any,
    both_ref, norm_ref,
    volt, seen, inc, partial, flow, stage, land, edge, coef, code_out, code, joint,
    v_ref, term_ref, cur_ref, chg_ref, src_ref, jac_ref, enc_ref, dec_ref, add_ref, part,
    v_send, v_recv, edge_send, edge_recv, core_send, core_recv, code_send, code_recv, back_send, back_recv,
    part_send, part_recv, load_sem,
):
    dom = lax.axis_index("dom")
    freq = lax.axis_index("freq")
    rows, nodes = v_ref.shape
    wide, elems = inc.shape
    border = seen.shape[2]
    chips = freqs // 2
    chip = freq // 2
    core = freq % 2
    other = 1 - core
    half = nodes // 2
    bw = min(2048, elems)
    ew = min(2048, elems)
    kb = 256
    one, zero = jnp.bfloat16(1.0), jnp.bfloat16(0.0)

    loads = [
        pltpu.make_async_copy(a, b, load_sem.at[i])
        for i, (a, b) in enumerate(
            (
                (term_any, term_ref), (v_any, v_ref), (cur_any, cur_ref), (chg_any, chg_ref),
                (enc_any.at[freq], enc_ref), (dec_any.at[chip], dec_ref), (add_any.at[chip], add_ref),
                (src_any, src_ref), (jac_any, jac_ref),
            )
        )
    ]
    for load in loads[:4]:
        load.start()

    barrier = pltpu.get_barrier_semaphore()
    for j in range(1, doms):
        pl.semaphore_signal(barrier, inc=1, device_id={"dom": xor(dom, j, doms)}, device_id_type=MESH)
    for j in range(1, chips):
        peer = xor(chip, j, chips) * 2 + core
        pl.semaphore_signal(barrier, inc=1, device_id={"freq": peer}, device_id_type=MESH)
    pl.semaphore_signal(barrier, inc=1, device_id={"freq": chip * 2 + other}, device_id_type=MESH)

    for load in loads[4:]:
        load.start()
    for load in loads[:2]:
        load.wait()

    def dom_copy(j, source, target, send, recv, sender):
        return pltpu.make_async_remote_copy(
            src_ref=source,
            dst_ref=target.at[sender],
            send_sem=send.at[j],
            recv_sem=recv.at[sender],
            device_id={"dom": xor(dom, j, doms)},
            device_id_type=MESH,
        )

    def v_copy(j, sender):
        return dom_copy(j, v_ref.at[:, :border], seen, v_send, v_recv, sender)

    def edge_copy(j, owner, sender):
        return dom_copy(j, edge_out(owner), edge, edge_send, edge_recv, sender)

    blocks = half // border
    direct = min(DIRECT, blocks) if relay else blocks
    inner = chip % 4 % 3 != 0
    if relay:
        joint_rank, merged_rank, width = relay

    def clear(ref, b, start, stop):
        if stop > start:
            ref[b, start:stop] = jnp.zeros((stop - start, border), jnp.float32)

    for b in range(blocks):
        clear(code, b, rank, stride)
        if b >= blocks - direct:
            for j in range(2, chips):
                clear(code, b, j * stride - stride + rank, j * stride)
            clear(code, b, (chips - 1) * stride, code.shape[1])
        else:
            clear(code, b, stride + merged_rank, code.shape[1])
            clear(joint, b, joint_rank, width)

    high, low = split(v_ref[...])
    volt[:rows, :nodes] = high
    volt[rows:, :nodes] = low

    def build(i, carry):
        @pl.when(i == 1)
        def _():
            pl.semaphore_wait(barrier, doms + chips - 1)
            for j in range(doms - 1, 0, -1):
                v_copy(j, dom).start()

        cols = pl.ds(pl.multiple_of(i * bw, bw), bw)
        first = term_ref[0:1, cols]
        second = term_ref[1:2, cols]
        same = first == second
        first = jnp.where(same, -1, first)
        second = jnp.where(same, -1, second)
        total = jnp.zeros((2 * rows, bw), jnp.float32)
        base = lax.broadcasted_iota(jnp.int16, (kb, bw), 0)
        for k in range(wide // kb):
            plus = base == (first - k * kb).astype(jnp.int16)
            minus = base == (second - k * kb).astype(jnp.int16)
            tile = jnp.where(plus, one, jnp.where(minus, -one, zero))
            inc[k * kb : (k + 1) * kb, cols] = tile
            if k * kb < nodes:
                total = total + dot(volt[:, k * kb : (k + 1) * kb], tile)
        partial[:, cols] = total[:rows] + total[rows:]
        return carry

    lax.fori_loop(0, elems // bw, build, 0)

    for load in loads[2:4]:
        load.wait()
    seen[dom] = v_ref[:, :border]
    for j in range(1, doms):
        v_copy(j, xor(dom, j, doms)).wait_recv()
    for p in range(doms):
        high, low = split(seen[p])
        volt[:rows, nodes + p * border : nodes + (p + 1) * border] = high
        volt[rows:, nodes + p * border : nodes + (p + 1) * border] = low

    def evaluate(i, carry):
        cols = pl.ds(pl.multiple_of(i * ew, ew), ew)
        total = dot(volt[:, nodes:], inc[nodes:, cols])
        across = partial[:, cols] + (total[:rows] + total[rows:])
        current = cur_ref[0:1, cols] * across + cur_ref[1:2, cols] * jnp.tanh(2.0 * across)
        charge = chg_ref[0:1, cols] * across + chg_ref[1:2, cols] * jnp.tanh(across)
        high, low = split(current)
        flow[:rows, cols] = high
        flow[rows : 2 * rows, cols] = low
        high, low = split(charge)
        flow[2 * rows : 3 * rows, cols] = high
        flow[3 * rows :, cols] = low
        return carry

    lax.fori_loop(0, elems // ew, evaluate, 0)

    own = 2 * rows

    def scatter(*starts):
        rows_at = [inc[pl.ds(pl.multiple_of(s, border), border), :] for s in starts]
        total = dot(flow[...], jnp.concatenate(rows_at, axis=0), ((1,), (1,)))
        current = total[:rows] + total[rows : 2 * rows]
        charge = total[2 * rows : 3 * rows] + total[3 * rows :]
        return jnp.concatenate([current, charge], axis=0)

    def edge_out(owner):
        cols = pl.ds(pl.multiple_of(owner % 2 * border, border), border)
        return stage.at[blocks + owner // 2, :, cols]

    def rows_of(which):
        return pl.ds(pl.multiple_of(which * rows, rows), rows)

    def columns_of(which, b):
        return pl.ds(pl.multiple_of(which * half + b * border, border), border)

    def core_copy(b):
        return pltpu.make_async_remote_copy(
            src_ref=stage.at[b, :, :border],
            dst_ref=land.at[b],
            send_sem=core_send.at[b],
            recv_sem=core_recv.at[b],
            device_id={"freq": chip * 2 + other},
            device_id_type=MESH,
        )

    def code_copy(b, j):
        piece = pl.ds((j - 1) * stride, rank)
        return pltpu.make_async_remote_copy(
            src_ref=code_out.at[b, piece],
            dst_ref=code.at[b, piece],
            send_sem=code_send.at[b, j],
            recv_sem=code_recv.at[b, j],
            device_id={"freq": xor(chip, j, chips) * 2 + core},
            device_id_type=MESH,
        )

    def send(b, source, target, count, send_at, recv_at, j):
        return pltpu.make_async_remote_copy(
            src_ref=code_out.at[b, pl.ds(source, count)],
            dst_ref=target,
            send_sem=code_send.at[b, send_at],
            recv_sem=code_recv.at[b, recv_at],
            device_id={"freq": xor(chip, j, chips) * 2 + core},
            device_id_type=MESH,
        )

    def joint_copy(b):
        return send(b, stride, joint.at[b, pl.ds(0, joint_rank)], joint_rank, 2, 3, 1)

    def merged_copy(b, i):
        target = code.at[b, pl.ds(stride, merged_rank)]
        return send(b, stride + i * width, target, merged_rank, 2 + i, 2, 3 - i)

    def back_copy(b, sender):
        return pltpu.make_async_remote_copy(
            src_ref=coef.at[b, rows_of(other)],
            dst_ref=both_ref.at[0, :, columns_of(sender, b)],
            send_sem=back_send.at[b],
            recv_sem=back_recv.at[b],
            device_id={"freq": chip * 2 + other},
            device_id_type=MESH,
        )

    def product(table, x):
        high, low = split(x)
        return dot(table, jnp.concatenate([high, low, high], axis=0))

    for load in loads[4:]:
        load.wait()

    far = sorted(range(1, chips), key=lambda j: -j)

    rims = doms // 2

    steps = blocks + rims
    ahead = blocks // 2 + 1

    lag = 3

    def is_block(i):
        return jnp.logical_and(jnp.logical_and(i >= 0, i < steps), jnp.logical_not(is_rim(i)))

    def is_rim(i):
        return jnp.logical_and(i >= ahead, i < ahead + rims)

    def block_of(i):
        return blocks - 1 - jnp.where(i < ahead, i, i - rims)

    def node_block(i, carry):
        rim = is_rim(i)
        b = block_of(i)
        edge_at = nodes + 2 * (i - ahead) * border

        @pl.when(i < steps)
        def _():
            there = jnp.where(rim, edge_at, other * half + b * border)
            here = jnp.where(rim, edge_at + border, core * half + b * border)
            stage[jnp.where(rim, blocks + i - ahead, b)] = scatter(there, here)

        @pl.when(i == ahead + rims - 1)
        def _():
            for k in range(doms - 1, 0, -1):
                edge_copy(k, xor(dom, k, doms), dom).start()

        @pl.when(i == steps - 1)
        def _():
            for k in range(1, doms):
                edge_copy(k, dom, xor(dom, k, doms)).wait_recv()
            cols = pl.ds(pl.multiple_of(other * border, border), border)
            total = stage[0, :, cols] + edge_out(dom)[...]
            for p in range(doms):
                total = total + jnp.where(dom == p, 0.0, edge[p])
            stage[0, :, cols] = total

        @pl.when(jnp.logical_and(i < steps, jnp.logical_not(rim)))
        def _():
            core_copy(b).start()

        done = block_of(i - 1)
        straight = done >= blocks - direct

        def flows():
            return jnp.concatenate([stage[done, :, border:], land[done]], axis=0)

        @pl.when(is_block(i - 1))
        def _():
            core_copy(done).wait_recv()
            mode = jnp.where(straight, 0, 1)
            result = product(enc_ref[mode], flows())
            coef[done] = result[:own]
            code_out[done] = result[own:]

            @pl.when(straight)
            def _():
                for j in far[:-1]:
                    code_copy(done, j).start()

            if direct < blocks:
                @pl.when(jnp.logical_not(jnp.logical_or(straight, inner)))
                def _():
                    joint_copy(done).start()

        if direct < blocks:
            old = block_of(i - 1 - lag)
            late = jnp.logical_and(is_block(i - 1 - lag), old < blocks - direct)

            @pl.when(jnp.logical_and(late, inner))
            def _():
                joint_copy(old).wait_recv()
                both = pl.ds(stride, 2 * width)
                code_out[old, both] = code_out[old, both] + product(add_ref[...], joint[old])
                for k in range(2):
                    merged_copy(old, k).start()

        @pl.when(is_block(i - 1 - lag))
        def _():
            code_copy(block_of(i - 1 - lag), 1).start()

        return carry

    lax.fori_loop(0, steps + 1 + lag, node_block, 0)

    def join(b):
        code_copy(b, 1).wait_recv()

        straight = b >= blocks - direct

        @pl.when(straight)
        def _():
            for j in far[:-1]:
                code_copy(b, j).wait_recv()

        if direct < blocks:
            @pl.when(jnp.logical_not(straight))
            def _():
                merged_copy(b, 0).wait_recv()

        mode = jnp.where(straight, 0, 1)
        coef[b] = coef[b] + product(dec_ref[mode], code[b])
        back_copy(b, core).start()
        both_ref[0, :, columns_of(core, b)] = coef[b, rows_of(core)]

    even = lax.broadcasted_iota(jnp.int32, (rows, LANES), 0) % 2 == 0

    def fold(x):
        return jnp.sum((x * x).reshape(rows // 8, 8, LANES), axis=0)

    def finish(b, sums):
        def piece(i, carry):
            @pl.when(i == 1)
            def _():
                back_copy(b, other).wait_recv()

            cols = columns_of(jnp.where(i == 1, other, core), b)
            residual = both_ref[0, :, cols] - src_ref[:, cols]
            upper = jnp.where(even, residual, pltpu.roll(residual, 1, 0))
            lower = jnp.where(even, pltpu.roll(residual, rows - 1, 0), residual)
            raw = -(jac_ref[:, 0, cols] * upper + jac_ref[:, 1, cols] * lower)
            both_ref[0, :, cols] = residual
            both_ref[1, :, cols] = raw
            return carry[0] + fold(raw), carry[1] + fold(residual)

        return lax.fori_loop(0, 2, piece, sums)

    zeros = jnp.zeros((8, LANES), jnp.float32)

    def close(i, sums):
        b = blocks - 1 - i
        join(b)
        return lax.cond(i > 0, lambda s: finish(b + 1, s), lambda s: s, sums)

    sums = finish(0, lax.fori_loop(0, blocks, close, (zeros, zeros)))

    def halves(x):
        return x + pltpu.roll(x, LANES // 2, 1)

    folded = jnp.where(
        lax.broadcasted_iota(jnp.int32, (8, LANES), 1) < LANES // 2, halves(sums[0]), halves(sums[1])
    )
    lane = lax.broadcasted_iota(jnp.int32, (1, LANES), 1)
    count = doms * freqs
    me = dom * freqs + freq
    part[me] = jnp.sum(folded, axis=0, keepdims=True)

    def part_copy(j, sending):
        dom_at, freq_at = xor(dom, j // freqs, doms), xor(freq, j % freqs, freqs)
        return pltpu.make_async_remote_copy(
            src_ref=part.at[me],
            dst_ref=part.at[me if sending else dom_at * freqs + freq_at],
            send_sem=part_send.at[j],
            recv_sem=part_recv.at[j],
            device_id={"dom": dom_at, "freq": freq_at},
            device_id_type=MESH,
        )

    for j in range(count - 1, 0, -1):
        part_copy(j, True).start()
    for j in range(count - 1, 0, -1):
        part_copy(j, False).wait_recv()
    total = jnp.sum(part[...], axis=0)
    raw_sum = jnp.sum(jnp.where(lane < LANES // 2, total, 0.0), axis=1, keepdims=True)
    res_sum = jnp.sum(jnp.where(lane < LANES // 2, 0.0, total), axis=1, keepdims=True)
    spread = jnp.sqrt(raw_sum / entries + 1e-06)
    both_ref[1] = both_ref[1] * jnp.minimum(1.0, trust_radius / spread)
    norm_ref[...] = jnp.sqrt(res_sum)

    for j in range(1, doms):
        v_copy(j, dom).wait_send()
        edge_copy(j, dom, dom).wait_send()

    for b in range(blocks):
        core_copy(b).wait_send()
        back_copy(b, core).wait_send()
        code_copy(b, 1).wait_send()
        if b >= blocks - direct:
            for j in far[:-1]:
                code_copy(b, j).wait_send()
        else:
            @pl.when(inner)
            def _():
                for k in range(2):
                    merged_copy(b, k).wait_send()

            @pl.when(jnp.logical_not(inner))
            def _():
                joint_copy(b).wait_send()

    for j in range(1, count):
        part_copy(j, True).wait_send()


def place_kernel(both_any, norm_any, residual_any, step_any, out_norm_any, sem):
    copies = [
        pltpu.make_async_copy(a, b, sem.at[i])
        for i, (a, b) in enumerate(
            ((both_any.at[0], residual_any), (both_any.at[1], step_any), (norm_any, out_norm_any))
        )
    ]
    for copy in copies:
        copy.start()
    for copy in copies:
        copy.wait()


def body(doms, freqs, voltages, sources, terminals, elem_current, elem_charge, jacobi):
    rows, nodes = voltages.shape
    elems = terminals.shape[1]
    border = nodes // 16
    wide = nodes + doms * border
    samples = rows * freqs
    chips = freqs // 2
    blocks = nodes // 2 // border
    own = 2 * rows
    f32, bf16 = jnp.float32, jnp.bfloat16
    dma = pltpu.SemaphoreType.DMA
    vmem = pl.BlockSpec(memory_space=VMEM)
    anywhere = pl.BlockSpec(memory_space=pl.ANY)
    tables, rank, stride, relay = exchange_tables(samples, chips)
    codes = (chips - 1) * stride
    width = relay[2] if relay else 16
    both, norm = pl.pallas_call(
        functools.partial(kernel, doms, freqs, float(samples * nodes * doms), rank, stride, relay),
        out_shape=(
            VMEM((2, rows, nodes), f32),
            jax.ShapeDtypeStruct((1, 1), f32),
        ),
        in_specs=[anywhere] * 9,
        out_specs=(vmem, vmem),
        scratch_shapes=[
            VMEM((2 * rows, wide), bf16),
            VMEM((doms, rows, border), f32),
            VMEM((wide, elems), bf16),
            VMEM((rows, elems), f32),
            VMEM((4 * rows, elems), bf16),
            VMEM((blocks + doms // 2, own, 2 * border), f32),
            VMEM((blocks, own, border), f32),
            VMEM((doms, own, border), f32),
            VMEM((blocks, own, border), f32),
            VMEM((blocks, max(codes, stride + 2 * width) if relay else codes, border), f32),
            VMEM((blocks, max(codes, stride + width) if relay else codes, border), f32),
            VMEM((blocks, width, border), f32),
            VMEM((rows, nodes), f32),
            VMEM((2, elems), jnp.int32),
            VMEM((2, elems), f32),
            VMEM((2, elems), f32),
            VMEM((rows, nodes), f32),
            VMEM((rows, 2, nodes), f32),
            *(VMEM(table.shape[1:], bf16) for table in tables),
            VMEM((doms * freqs, 1, LANES), f32),
            dma((doms,)), dma((doms,)),
            dma((doms,)), dma((doms,)),
            dma((blocks,)), dma((blocks,)),
            dma((blocks, chips)), dma((blocks, chips)),
            dma((blocks,)), dma((blocks,)),
            dma((doms * freqs,)), dma((doms * freqs,)),
            dma((9,)),
        ],
        compiler_params=pltpu.CompilerParams(
            collective_id=0, has_side_effects=True, vmem_limit_bytes=56 * 1024 * 1024
        ),
    )(
        voltages, terminals, elem_current, elem_charge,
        sources, jacobi.reshape(rows, 2, nodes), *map(jnp.asarray, tables),
    )
    residual, step, norm = pl.pallas_call(
        place_kernel,
        out_shape=(
            jax.ShapeDtypeStruct((rows, nodes), f32),
            jax.ShapeDtypeStruct((rows, nodes), f32),
            jax.ShapeDtypeStruct((1, 1), f32),
        ),
        in_specs=[anywhere] * 2,
        out_specs=(anywhere,) * 3,
        scratch_shapes=[dma((3,))],
        compiler_params=pltpu.CompilerParams(vmem_limit_bytes=1024 * 1024),
    )(both, norm)
    return residual, step, norm.reshape(())


def solution(mesh):
    placed = (
        P("freq", "dom"),
        P("freq", "dom"),
        P(None, "dom"),
        P(None, "dom"),
        P(None, "dom"),
        P("freq", None, None, "dom"),
    )
    return jax.shard_map(
        functools.partial(body, mesh.shape["dom"], mesh.shape["freq"]),
        mesh=mesh,
        in_specs=placed,
        out_specs=(P("freq", "dom"), P("freq", "dom"), P()),
        check_vma=False,
    )
```

```python
import functools
import math

import jax
import jax.numpy as jnp
import numpy as np
from jax import lax
from jax.experimental import pallas as pl
from jax.experimental.pallas import tpu as pltpu
from jax.sharding import PartitionSpec as P

MESH = pl.DeviceIdType.MESH
LANES = 128
VMEM = pltpu.VMEM
trust_radius = 2.0
TOLERANCE = 6e-7
DIRECT = 2


def fourier_tables(samples):
    row = np.arange(samples)
    harmonic = row // 2
    sine = row % 2 == 1
    order = np.where(harmonic == 0, np.where(sine, samples // 2, 0), harmonic)
    phase = (order[:, None] * np.arange(samples)[None, :] % samples) * (2.0 * math.pi / samples)
    values = np.where((sine & (harmonic > 0))[:, None], np.sin(phase), np.cos(phase))
    weight = np.where(harmonic == 0, math.sqrt(1.0 / samples), math.sqrt(2.0 / samples))
    full = values * weight[:, None]
    pairs = full.reshape(samples // 2, 2, samples)
    rate = (2.0 / samples) * np.arange(samples // 2)
    derived = np.stack([pairs[:, 1], -pairs[:, 0]], axis=1) * rate[:, None, None]
    return full, derived.reshape(samples, samples)


def split_table(full):
    full = full.astype(np.float32)
    high = full.astype(jnp.bfloat16)
    low = (full - high.astype(np.float32)).astype(jnp.bfloat16)
    return np.concatenate([high, high, low], axis=-1)


def up(value, step):
    return -(-value // step) * step


def exchange_tables(samples, chips):
    full, derived = fourier_tables(samples)
    own = samples // chips
    part = own // 2
    blocks, rank = {}, 0
    for k in range(chips):
        for m in range(chips):
            rows, first, second = slice(m * own, (m + 1) * own), k * own, k * own + part
            block = np.concatenate(
                [t[rows, s : s + part] for s in (first, second) for t in (full, derived)], axis=1
            )
            blocks[m, k] = block
            if m != k:
                values = np.linalg.svd(block, compute_uv=False)
                rank = max(rank, int((values > TOLERANCE * values[0]).sum()))
    rank = up(rank, 8)
    stride = up(rank, 16)
    encode = np.zeros((chips, 2, own + (chips - 1) * stride, 2 * own))
    decode = np.zeros((chips, own, (chips - 1) * stride))
    for k in range(chips):
        encode[k, :, :own] = blocks[k, k]
        for j in range(1, chips):
            start = (j - 1) * stride
            left, values, right = np.linalg.svd(blocks[k ^ j, k], full_matrices=False)
            encode[k, :, own + start : own + start + rank] = values[:rank, None] * right[:rank]
            decode[k ^ j, :, start : start + rank] = left[:, :rank]
    relayed = relay_tables(blocks, encode, decode, rank, stride) if chips == 4 else None
    tables = [per_core(encode)[:, None], decode[:, None], np.zeros((chips, 16, LANES))]
    if relayed is not None:
        enc, dec, add = relayed[0]
        tables = [both_modes(per_core(encode), enc, 1), both_modes(decode, dec, 2), add]
    flat = [split_table(table) for table in tables]
    return flat, rank, stride, relayed[1:] if relayed is not None else None


def per_core(encode):
    own = encode.shape[3] // 2
    encode = encode.copy()
    encode[:, 1] = np.roll(encode[:, 1], own, axis=2)
    return encode.reshape((-1,) + encode.shape[2:])


def both_modes(first, second, axis):
    size = max(first.shape[axis], second.shape[axis])
    pads = [[(0, size - t.shape[i] if i == axis else 0) for i in range(3)] for t in (first, second)]
    return np.stack([np.pad(first, pads[0]), np.pad(second, pads[1])], axis=1)


def factor(block):
    left, values, right = np.linalg.svd(block, full_matrices=False)
    return left, values[:, None] * right, int((values > TOLERANCE * values[0]).sum())


def relay_tables(blocks, encode, decode, rank, stride):
    own = decode.shape[1]
    lines = ((0, 1, 2, 3), (3, 2, 1, 0))
    joint, merged = {}, {}
    for outer, inner, *far in lines:
        joint[inner] = factor(np.concatenate([blocks[d, outer] for d in far], axis=0))
        for d in far:
            merged[d] = factor(np.concatenate([blocks[d, inner], blocks[d, outer]], axis=1))
    joint_rank = up(max(j[2] for j in joint.values()), 8)
    merged_rank = up(max(m[2] for m in merged.values()), 8)
    width = up(max(joint_rank, merged_rank), 16)
    enc = np.zeros((4, 2, own + stride + 2 * width, 2 * own))
    dec = np.zeros((4, own, stride + width))
    add = np.zeros((4, 2 * width, width))
    enc[:, :, : own + stride] = encode[:, :, : own + stride]
    dec[:, :, :stride] = decode[:, :, :stride]
    start = own + stride
    for outer, inner, *far in lines:
        left, right, _ = joint[inner]
        enc[outer, :, start : start + joint_rank] = right[:joint_rank]
        for i, d in enumerate(far):
            basis = merged[d][0][:, :merged_rank]
            rows = slice(i * width, i * width + merged_rank)
            enc[inner, :, start + rows.start : start + rows.stop] = basis.T @ blocks[d, inner]
            add[inner, rows, :joint_rank] = basis.T @ left[i * own : (i + 1) * own, :joint_rank]
            dec[d, :, stride : stride + merged_rank] = basis
    return [per_core(enc), dec, add], joint_rank, merged_rank, width


def split(x):
    high = x.astype(jnp.bfloat16)
    low = (x - high.astype(jnp.float32)).astype(jnp.bfloat16)
    return high, low


def dot(a, b, contract=((1,), (0,))):
    return lax.dot_general(a, b, (contract, ((), ())), preferred_element_type=jnp.float32)


def xor(a, b, count):
    out, bit = 0, 1
    while bit < count:
        out = out + bit * ((a // bit + b // bit) % 2)
        bit *= 2
    return out


def kernel(
    doms, freqs, entries, rank, stride, relay,
    v_any, term_any, cur_any, chg_any, src_any, jac_any,
    enc_any, dec_any, add_any,
    both_ref, norm_ref,
    volt, seen, inc, partial, flow, stage, land, edge, coef, code_out, code, joint,
    v_ref, term_ref, cur_ref, chg_ref, src_ref, jac_ref, enc_ref, dec_ref, add_ref, part,
    v_send, v_recv, edge_send, edge_recv, core_send, core_recv, code_send, code_recv, back_send, back_recv,
    part_send, part_recv, load_sem,
):
    dom = lax.axis_index("dom")
    freq = lax.axis_index("freq")
    rows, nodes = v_ref.shape
    wide, elems = inc.shape
    border = seen.shape[2]
    chips = freqs // 2
    chip = freq // 2
    core = freq % 2
    other = 1 - core
    half = nodes // 2
    bw = min(2048, elems)
    ew = min(4096, elems)
    kb = 256
    one, zero = jnp.bfloat16(1.0), jnp.bfloat16(0.0)

    loads = [
        pltpu.make_async_copy(a, b, load_sem.at[i])
        for i, (a, b) in enumerate(
            (
                (term_any, term_ref), (v_any, v_ref), (cur_any, cur_ref), (chg_any, chg_ref),
                (enc_any.at[freq], enc_ref), (dec_any.at[chip], dec_ref), (add_any.at[chip], add_ref),
                (src_any, src_ref), (jac_any, jac_ref),
            )
        )
    ]
    for load in loads[:4]:
        load.start()

    barrier = pltpu.get_barrier_semaphore()
    for j in range(1, doms):
        pl.semaphore_signal(barrier, inc=1, device_id={"dom": xor(dom, j, doms)}, device_id_type=MESH)
    for j in range(1, chips):
        peer = xor(chip, j, chips) * 2 + core
        pl.semaphore_signal(barrier, inc=1, device_id={"freq": peer}, device_id_type=MESH)
    pl.semaphore_signal(barrier, inc=1, device_id={"freq": chip * 2 + other}, device_id_type=MESH)

    for load in loads[4:]:
        load.start()
    for load in loads[:2]:
        load.wait()

    def dom_copy(j, source, target, send, recv, sender):
        return pltpu.make_async_remote_copy(
            src_ref=source,
            dst_ref=target.at[sender],
            send_sem=send.at[j],
            recv_sem=recv.at[sender],
            device_id={"dom": xor(dom, j, doms)},
            device_id_type=MESH,
        )

    def v_copy(j, sender):
        return dom_copy(j, v_ref.at[:, :border], seen, v_send, v_recv, sender)

    def edge_copy(j, owner, sender):
        return dom_copy(j, edge_out(owner), edge, edge_send, edge_recv, sender)

    blocks = half // border
    direct = min(DIRECT, blocks) if relay else blocks
    inner = chip % 4 % 3 != 0
    if relay:
        joint_rank, merged_rank, width = relay

    def clear(ref, b, start, stop):
        if stop > start:
            ref[b, start:stop] = jnp.zeros((stop - start, border), jnp.float32)

    for b in range(blocks):
        clear(code, b, rank, stride)
        if b >= blocks - direct:
            for j in range(2, chips):
                clear(code, b, j * stride - stride + rank, j * stride)
            clear(code, b, (chips - 1) * stride, code.shape[1])
        else:
            clear(code, b, stride + merged_rank, code.shape[1])
            clear(joint, b, joint_rank, width)

    high, low = split(v_ref[...])
    volt[:rows, :nodes] = high
    volt[rows:, :nodes] = low

    def build(i, carry):
        @pl.when(i == 1)
        def _():
            pl.semaphore_wait(barrier, doms + chips - 1)
            for j in range(doms - 1, 0, -1):
                v_copy(j, dom).start()

        cols = pl.ds(pl.multiple_of(i * bw, bw), bw)
        first = term_ref[0:1, cols]
        second = term_ref[1:2, cols]
        same = first == second
        first = jnp.where(same, -1, first)
        second = jnp.where(same, -1, second)
        total = jnp.zeros((2 * rows, bw), jnp.float32)
        base = lax.broadcasted_iota(jnp.int16, (kb, bw), 0)
        for k in range(wide // kb):
            plus = base == (first - k * kb).astype(jnp.int16)
            minus = base == (second - k * kb).astype(jnp.int16)
            tile = jnp.where(plus, one, jnp.where(minus, -one, zero))
            inc[k * kb : (k + 1) * kb, cols] = tile
            if k * kb < nodes:
                total = total + dot(volt[:, k * kb : (k + 1) * kb], tile)
        partial[:, cols] = total[:rows] + total[rows:]
        return carry

    lax.fori_loop(0, elems // bw, build, 0)

    for load in loads[2:4]:
        load.wait()
    seen[dom] = v_ref[:, :border]
    for j in range(1, doms):
        v_copy(j, xor(dom, j, doms)).wait_recv()
    for p in range(doms):
        high, low = split(seen[p])
        volt[:rows, nodes + p * border : nodes + (p + 1) * border] = high
        volt[rows:, nodes + p * border : nodes + (p + 1) * border] = low

    def evaluate(i, carry):
        cols = pl.ds(pl.multiple_of(i * ew, ew), ew)
        total = dot(volt[:, nodes:], inc[nodes:, cols])
        across = partial[:, cols] + (total[:rows] + total[rows:])
        current = cur_ref[0:1, cols] * across + cur_ref[1:2, cols] * jnp.tanh(2.0 * across)
        charge = chg_ref[0:1, cols] * across + chg_ref[1:2, cols] * jnp.tanh(across)
        high, low = split(current)
        flow[:rows, cols] = high
        flow[rows : 2 * rows, cols] = low
        high, low = split(charge)
        flow[2 * rows : 3 * rows, cols] = high
        flow[3 * rows :, cols] = low
        return carry

    lax.fori_loop(0, elems // ew, evaluate, 0)

    own = 2 * rows

    def scatter(*starts):
        rows_at = [inc[pl.ds(pl.multiple_of(s, border), border), :] for s in starts]
        total = dot(flow[...], jnp.concatenate(rows_at, axis=0), ((1,), (1,)))
        current = total[:rows] + total[rows : 2 * rows]
        charge = total[2 * rows : 3 * rows] + total[3 * rows :]
        return jnp.concatenate([current, charge], axis=0)

    def edge_out(owner):
        cols = pl.ds(pl.multiple_of(owner % 2 * border, border), border)
        return stage.at[blocks + owner // 2, :, cols]

    def rows_of(which):
        return pl.ds(pl.multiple_of(which * rows, rows), rows)

    def columns_of(which, b):
        return pl.ds(pl.multiple_of(which * half + b * border, border), border)

    def core_copy(b):
        return pltpu.make_async_remote_copy(
            src_ref=stage.at[b, :, :border],
            dst_ref=land.at[b],
            send_sem=core_send.at[b],
            recv_sem=core_recv.at[b],
            device_id={"freq": chip * 2 + other},
            device_id_type=MESH,
        )

    def code_copy(b, j):
        piece = pl.ds((j - 1) * stride, rank)
        return pltpu.make_async_remote_copy(
            src_ref=code_out.at[b, piece],
            dst_ref=code.at[b, piece],
            send_sem=code_send.at[b, j],
            recv_sem=code_recv.at[b, j],
            device_id={"freq": xor(chip, j, chips) * 2 + core},
            device_id_type=MESH,
        )

    def send(b, source, target, count, send_at, recv_at, j):
        return pltpu.make_async_remote_copy(
            src_ref=code_out.at[b, pl.ds(source, count)],
            dst_ref=target,
            send_sem=code_send.at[b, send_at],
            recv_sem=code_recv.at[b, recv_at],
            device_id={"freq": xor(chip, j, chips) * 2 + core},
            device_id_type=MESH,
        )

    def joint_copy(b):
        return send(b, stride, joint.at[b, pl.ds(0, joint_rank)], joint_rank, 2, 3, 1)

    def merged_copy(b, i):
        target = code.at[b, pl.ds(stride, merged_rank)]
        return send(b, stride + i * width, target, merged_rank, 2 + i, 2, 3 - i)

    def back_copy(b, sender):
        return pltpu.make_async_remote_copy(
            src_ref=coef.at[b, rows_of(other)],
            dst_ref=both_ref.at[0, :, columns_of(sender, b)],
            send_sem=back_send.at[b],
            recv_sem=back_recv.at[b],
            device_id={"freq": chip * 2 + other},
            device_id_type=MESH,
        )

    def product(table, x):
        high, low = split(x)
        return dot(table, jnp.concatenate([high, low, high], axis=0))

    for load in loads[4:]:
        load.wait()

    far = sorted(range(1, chips), key=lambda j: -j)

    rims = doms // 2

    steps = blocks + rims
    ahead = blocks // 2 + 1

    lag = 3

    def is_block(i):
        return jnp.logical_and(jnp.logical_and(i >= 0, i < steps), jnp.logical_not(is_rim(i)))

    def is_rim(i):
        return jnp.logical_and(i >= ahead, i < ahead + rims)

    def block_of(i):
        return blocks - 1 - jnp.where(i < ahead, i, i - rims)

    def node_block(i, carry):
        rim = is_rim(i)
        b = block_of(i)
        edge_at = nodes + 2 * (i - ahead) * border

        @pl.when(i < steps)
        def _():
            there = jnp.where(rim, edge_at, other * half + b * border)
            here = jnp.where(rim, edge_at + border, core * half + b * border)
            stage[jnp.where(rim, blocks + i - ahead, b)] = scatter(there, here)

        @pl.when(i == ahead + rims - 1)
        def _():
            for k in range(doms - 1, 0, -1):
                edge_copy(k, xor(dom, k, doms), dom).start()

        @pl.when(i == steps - 1)
        def _():
            for k in range(1, doms):
                edge_copy(k, dom, xor(dom, k, doms)).wait_recv()
            cols = pl.ds(pl.multiple_of(other * border, border), border)
            total = stage[0, :, cols] + edge_out(dom)[...]
            for p in range(doms):
                total = total + jnp.where(dom == p, 0.0, edge[p])
            stage[0, :, cols] = total

        @pl.when(jnp.logical_and(i < steps, jnp.logical_not(rim)))
        def _():
            core_copy(b).start()

        done = block_of(i - 1)
        straight = done >= blocks - direct

        def flows():
            return jnp.concatenate([stage[done, :, border:], land[done]], axis=0)

        if direct < blocks:
            old = block_of(i - 1 - lag)
            late = jnp.logical_and(is_block(i - 1 - lag), old < blocks - direct)

            @pl.when(jnp.logical_and(late, inner))
            def _():
                joint_copy(old).wait_recv()
                both = pl.ds(stride, 2 * width)
                code_out[old, both] = code_out[old, both] + product(add_ref[...], joint[old])
                for k in range(2):
                    merged_copy(old, k).start()

        @pl.when(is_block(i - 1))
        def _():
            core_copy(done).wait_recv()
            mode = jnp.where(straight, 0, 1)
            result = product(enc_ref[mode], flows())
            coef[done] = result[:own]
            code_out[done] = result[own:]

            @pl.when(straight)
            def _():
                for j in far[:-1]:
                    code_copy(done, j).start()

            if direct < blocks:
                @pl.when(jnp.logical_not(jnp.logical_or(straight, inner)))
                def _():
                    joint_copy(done).start()

        @pl.when(is_block(i - 1 - lag))
        def _():
            code_copy(block_of(i - 1 - lag), 1).start()

        return carry

    lax.fori_loop(0, steps + 1 + lag, node_block, 0)

    def join(b):
        code_copy(b, 1).wait_recv()

        straight = b >= blocks - direct

        @pl.when(straight)
        def _():
            for j in far[:-1]:
                code_copy(b, j).wait_recv()

        if direct < blocks:
            @pl.when(jnp.logical_not(straight))
            def _():
                merged_copy(b, 0).wait_recv()

        mode = jnp.where(straight, 0, 1)
        coef[b] = coef[b] + product(dec_ref[mode], code[b])
        back_copy(b, core).start()
        both_ref[0, :, columns_of(core, b)] = coef[b, rows_of(core)]

    even = lax.broadcasted_iota(jnp.int32, (rows, LANES), 0) % 2 == 0

    def fold(x):
        return jnp.sum((x * x).reshape(rows // 8, 8, LANES), axis=0)

    def finish(b, sums):
        def piece(i, carry):
            @pl.when(i == 1)
            def _():
                back_copy(b, other).wait_recv()

            cols = columns_of(jnp.where(i == 1, other, core), b)
            residual = both_ref[0, :, cols] - src_ref[:, cols]
            upper = jnp.where(even, residual, pltpu.roll(residual, 1, 0))
            lower = jnp.where(even, pltpu.roll(residual, rows - 1, 0), residual)
            raw = -(jac_ref[:, 0, cols] * upper + jac_ref[:, 1, cols] * lower)
            both_ref[0, :, cols] = residual
            both_ref[1, :, cols] = raw
            return carry[0] + fold(raw), carry[1] + fold(residual)

        return lax.fori_loop(0, 2, piece, sums)

    zeros = jnp.zeros((8, LANES), jnp.float32)

    def close(i, sums):
        b = blocks - 1 - i
        join(b)
        return lax.cond(i > 0, lambda s: finish(b + 1, s), lambda s: s, sums)

    sums = finish(0, lax.fori_loop(0, blocks, close, (zeros, zeros)))

    def halves(x):
        return x + pltpu.roll(x, LANES // 2, 1)

    folded = jnp.where(
        lax.broadcasted_iota(jnp.int32, (8, LANES), 1) < LANES // 2, halves(sums[0]), halves(sums[1])
    )
    lane = lax.broadcasted_iota(jnp.int32, (1, LANES), 1)
    count = doms * freqs
    me = dom * freqs + freq
    part[me] = jnp.sum(folded, axis=0, keepdims=True)

    def part_copy(j, sending):
        dom_at, freq_at = xor(dom, j // freqs, doms), xor(freq, j % freqs, freqs)
        return pltpu.make_async_remote_copy(
            src_ref=part.at[me],
            dst_ref=part.at[me if sending else dom_at * freqs + freq_at],
            send_sem=part_send.at[j],
            recv_sem=part_recv.at[j],
            device_id={"dom": dom_at, "freq": freq_at},
            device_id_type=MESH,
        )

    for j in range(count - 1, 0, -1):
        part_copy(j, True).start()
    for j in range(count - 1, 0, -1):
        part_copy(j, False).wait_recv()
    total = jnp.sum(part[...], axis=0)
    raw_sum = jnp.sum(jnp.where(lane < LANES // 2, total, 0.0), axis=1, keepdims=True)
    res_sum = jnp.sum(jnp.where(lane < LANES // 2, 0.0, total), axis=1, keepdims=True)
    spread = jnp.sqrt(raw_sum / entries + 1e-06)
    both_ref[1] = both_ref[1] * jnp.minimum(1.0, trust_radius / spread)
    norm_ref[...] = jnp.sqrt(res_sum)

    for j in range(1, doms):
        v_copy(j, dom).wait_send()
        edge_copy(j, dom, dom).wait_send()

    for b in range(blocks):
        core_copy(b).wait_send()
        back_copy(b, core).wait_send()
        code_copy(b, 1).wait_send()
        if b >= blocks - direct:
            for j in far[:-1]:
                code_copy(b, j).wait_send()
        else:
            @pl.when(inner)
            def _():
                for k in range(2):
                    merged_copy(b, k).wait_send()

            @pl.when(jnp.logical_not(inner))
            def _():
                joint_copy(b).wait_send()

    for j in range(1, count):
        part_copy(j, True).wait_send()


def place_kernel(both_any, norm_any, residual_any, step_any, out_norm_any, sem):
    copies = [
        pltpu.make_async_copy(a, b, sem.at[i])
        for i, (a, b) in enumerate(
            ((both_any.at[0], residual_any), (both_any.at[1], step_any), (norm_any, out_norm_any))
        )
    ]
    for copy in copies:
        copy.start()
    for copy in copies:
        copy.wait()


def body(doms, freqs, voltages, sources, terminals, elem_current, elem_charge, jacobi):
    rows, nodes = voltages.shape
    elems = terminals.shape[1]
    border = nodes // 16
    wide = nodes + doms * border
    samples = rows * freqs
    chips = freqs // 2
    blocks = nodes // 2 // border
    own = 2 * rows
    f32, bf16 = jnp.float32, jnp.bfloat16
    dma = pltpu.SemaphoreType.DMA
    vmem = pl.BlockSpec(memory_space=VMEM)
    anywhere = pl.BlockSpec(memory_space=pl.ANY)
    tables, rank, stride, relay = exchange_tables(samples, chips)
    codes = (chips - 1) * stride
    width = relay[2] if relay else 16
    both, norm = pl.pallas_call(
        functools.partial(kernel, doms, freqs, float(samples * nodes * doms), rank, stride, relay),
        out_shape=(
            VMEM((2, rows, nodes), f32),
            jax.ShapeDtypeStruct((1, 1), f32),
        ),
        in_specs=[anywhere] * 9,
        out_specs=(vmem, vmem),
        scratch_shapes=[
            VMEM((2 * rows, wide), bf16),
            VMEM((doms, rows, border), f32),
            VMEM((wide, elems), bf16),
            VMEM((rows, elems), f32),
            VMEM((4 * rows, elems), bf16),
            VMEM((blocks + doms // 2, own, 2 * border), f32),
            VMEM((blocks, own, border), f32),
            VMEM((doms, own, border), f32),
            VMEM((blocks, own, border), f32),
            VMEM((blocks, max(codes, stride + 2 * width) if relay else codes, border), f32),
            VMEM((blocks, max(codes, stride + width) if relay else codes, border), f32),
            VMEM((blocks, width, border), f32),
            VMEM((rows, nodes), f32),
            VMEM((2, elems), jnp.int32),
            VMEM((2, elems), f32),
            VMEM((2, elems), f32),
            VMEM((rows, nodes), f32),
            VMEM((rows, 2, nodes), f32),
            *(VMEM(table.shape[1:], bf16) for table in tables),
            VMEM((doms * freqs, 1, LANES), f32),
            dma((doms,)), dma((doms,)),
            dma((doms,)), dma((doms,)),
            dma((blocks,)), dma((blocks,)),
            dma((blocks, chips)), dma((blocks, chips)),
            dma((blocks,)), dma((blocks,)),
            dma((doms * freqs,)), dma((doms * freqs,)),
            dma((9,)),
        ],
        compiler_params=pltpu.CompilerParams(
            collective_id=0, has_side_effects=True, vmem_limit_bytes=56 * 1024 * 1024
        ),
    )(
        voltages, terminals, elem_current, elem_charge,
        sources, jacobi.reshape(rows, 2, nodes), *map(jnp.asarray, tables),
    )
    residual, step, norm = pl.pallas_call(
        place_kernel,
        out_shape=(
            jax.ShapeDtypeStruct((rows, nodes), f32),
            jax.ShapeDtypeStruct((rows, nodes), f32),
            jax.ShapeDtypeStruct((1, 1), f32),
        ),
        in_specs=[anywhere] * 2,
        out_specs=(anywhere,) * 3,
        scratch_shapes=[dma((3,))],
        compiler_params=pltpu.CompilerParams(vmem_limit_bytes=1024 * 1024),
    )(both, norm)
    return residual, step, norm.reshape(())


def solution(mesh):
    placed = (
        P("freq", "dom"),
        P("freq", "dom"),
        P(None, "dom"),
        P(None, "dom"),
        P(None, "dom"),
        P("freq", None, None, "dom"),
    )
    return jax.shard_map(
        functools.partial(body, mesh.shape["dom"], mesh.shape["freq"]),
        mesh=mesh,
        in_specs=placed,
        out_specs=(P("freq", "dom"), P("freq", "dom"), P()),
        check_vma=False,
    )
```
